768 devices in a mesh: shard: 12 (over z), group: 64 (over x, y, core).
Axes of the slice: x: 4, y: 8, z: 12, core: 2. Of those that a mesh axis runs over, the one named last changes fastest.
Arguments:
- item_ids: int32 [98304], P(('shard', 'group')), may hold values from 0 to 8191, as said below
- seq_lengths: int32 [768, 8], P(('shard', 'group')), may hold values from 1 to 64, 128 in all within a row
- time_buckets: int32 [98304], P(('shard', 'group')), may hold values from 0 to 63
- neg_ids: int32 [12, 2048], P('shard', 'group'), may hold values from 0 to 8191, as said below
- table: float32 [8192, 512], P('group'), may hold values from -6 to 6
- w_in: float32 [512, 2048], replicated, may hold values from -0.25 to 0.25
- b_in: float32 [2048], replicated, may hold values from -3 to 3
- w_out: float32 [512, 512], replicated, may hold values from -0.25 to 0.25
- rab: float32 [4, 64], replicated, may hold values from -4 to 4
Outputs:
- table_grad: float32 [8192, 512], P('group')
- token_loss: float32 [98304], P(('shard', 'group'))
The draws below stay inside these ranges and needn't reach their ends.
Inputs may be any that keep to these rules, and one draw needn't show every extreme that they name: `item_ids`: item i is held by the rows of group index i // 128. The 128 tokens of one device name items of any one group index at most 4 times; in every draw, for each shard index, one group index is named exactly 4 times by every device of that shard index. `neg_ids`: entry r of a row names an item of group index r // 32.
All inputs are finite; a program needn't handle non-finite values.
Results may differ from the reference program's by a relative error of at most 0.0003.
Values sent between devices are 32-bit elements; how exact they have to be, the bound alone decides.
A program may use at most 64 MiB of HBM per device.

```python
import math
import jax
import jax.numpy as jnp
import numpy as np
from jax import lax

D = 512
HEADS = 4
NB = 64
TOK_DEV = 128
SEQ_DEV = 8
MOST_LEN = 64
ROWS_DEV = 128
NEG_DEV = 32
NEG = 2048
CAP = 4
ITEMS = 8192
TOKENS = 98304
N_SHARD = 12
N_GROUP = 64


def draw_item_ids(key, part):
    slots = N_GROUP * CAP
    devices = N_SHARD * N_GROUP
    hot_key, dev_key = jax.random.split(jax.random.fold_in(key, 11))
    hot = jax.random.randint(hot_key, (N_SHARD,), 0, N_GROUP)

    def one(dkey, hot_owner):
        first, second, third = jax.random.split(dkey, 3)
        order = jax.random.permutation(first, slots)
        owners = order // CAP
        rank = jnp.argsort((owners != hot_owner).astype(jnp.int32), stable=True)
        chosen = jax.random.permutation(second, owners[rank][:TOK_DEV])
        rows = jax.random.randint(third, (TOK_DEV,), 0, ROWS_DEV)
        return chosen * ROWS_DEV + rows
    keys = jax.random.split(dev_key, devices)
    hots = jnp.repeat(hot, N_GROUP)
    return jax.vmap(one)(keys, hots).reshape(-1).astype(jnp.int32)


def draw_neg_ids(key, part):
    column = jnp.arange(NEG, dtype=jnp.int32)
    rows = jax.random.randint(jax.random.fold_in(key, 23), (N_SHARD, NEG), 0, ROWS_DEV)
    return ((column // NEG_DEV)[None, :] * ROWS_DEV + rows).astype(jnp.int32)


def touch_ends(result, key, low, top_value):
    longest = result.shape.index(max(result.shape))
    spots = []
    for shift in (0, 1):
        where = [jax.random.randint(jax.random.fold_in(key, axis), (), 0, length) for axis, length in enumerate(result.shape)]
        where[longest] = (where[longest] + shift) % result.shape[longest]
        spots.append(tuple(where))
    return result.at[spots[0]].set(low).at[spots[1]].set(top_value)


def level_of(own_key, shape, shards, least, high):
    loudness = 1.0
    for dim, parts in shards:
        heights = jax.random.uniform(jax.random.fold_in(jax.random.fold_in(own_key, 6), dim), (parts,), jnp.float32, least / len(shards), high / len(shards))
        loudness = loudness * jnp.repeat(jnp.exp(heights), shape[dim] // parts).reshape((-1,) + (1,) * (len(shape) - 1 - dim))
    return loudness


def split_up(amount, total, most, slope):
    weights = [(1 << 20) // math.isqrt(standing ** slope) + 1 for standing in range(2, amount + 1)]
    rest, holding = total - most - (amount - 1), [1] * (amount - 1)
    while rest > 0:
        free = [i for i in range(amount - 1) if holding[i] < most]
        pool, remaining = sum([weights[i] for i in free]), rest
        for i in free:
            extra = min(most - holding[i], max(1, remaining * weights[i] // pool), rest)
            holding[i] = holding[i] + extra
            rest = rest - extra
    return np.array([most] + holding)


def ragged_sizes(rng, number_of, total, limit, lean):
    if number_of == 2:
        one = jax.random.randint(rng, (), max(1, total - limit), min(limit, total - 1) + 1)
        return jnp.stack([one, total - one])
    tallies = jnp.asarray(split_up(number_of, total, limit, lean), jnp.int32)
    twos = (number_of - 1) // 2
    donor, taker = tallies[1:1 + 2 * twos:2], tallies[2:2 + 2 * twos:2]
    room = jnp.minimum(donor - 1, limit - taker)
    shifted = jax.random.randint(jax.random.fold_in(rng, 1), (twos,), 0, 1 << 20) % (room + 1)
    tallies = tallies.at[1:1 + 2 * twos:2].set(donor - shifted).at[2:2 + 2 * twos:2].set(taker + shifted)
    return tallies[jax.random.permutation(jax.random.fold_in(rng, 2), number_of)]


def gaussian(key, shape, scale, reach, cuts=(), kind=jnp.bfloat16):
    level = level_of(key, shape, cuts, -0.22, 0.18) if cuts else 1.0
    array = jax.random.normal(key, shape, jnp.float32) * scale * level
    return jnp.minimum(jnp.maximum(array, -reach), reach).astype(kind)


def setup_inputs(seed: int = 0) -> dict:
    key_of = jax.random.split(jax.random.key(seed), 10)
    item_ids = draw_item_ids(jax.random.fold_in(key_of[9], 71), 0)
    seq_lengths = jax.vmap(lambda own: ragged_sizes(own, SEQ_DEV, TOK_DEV, MOST_LEN, 2))(jax.random.split(key_of[1], (N_SHARD * N_GROUP))).reshape((N_SHARD * N_GROUP, SEQ_DEV)).astype(jnp.int32)
    time_buckets = touch_ends(jax.random.randint(key_of[2], (TOKENS,), 0, NB), jax.random.fold_in(key_of[2], 1), 0, NB - 1).astype(jnp.int32)
    neg_ids = draw_neg_ids(jax.random.fold_in(key_of[9], 71), 0)
    table = gaussian(key_of[4], (ITEMS, D), 1.0, 6.0, ((0, 64),), jnp.float32)
    w_in = gaussian(key_of[5], (D, 4 * D), D ** -0.5, 0.25, (), jnp.float32)
    b_in = gaussian(key_of[6], (4 * D,), 0.5, 3.0, (), jnp.float32)
    w_out = gaussian(key_of[7], (D, D), D ** -0.5, 0.25, (), jnp.float32)
    rab = gaussian(key_of[8], (HEADS, NB), 1.0, 4.0, (), jnp.float32)
    return dict(item_ids=item_ids, seq_lengths=seq_lengths, time_buckets=time_buckets, neg_ids=neg_ids, table=table, w_in=w_in, b_in=b_in, w_out=w_out, rab=rab)


HIGH = lax.Precision.HIGHEST
TEMPER = 0.05

def layer_norm(value):
    mean = lax.optimization_barrier(jnp.mean(value, -1, keepdims=True))
    centered = value - mean
    var = lax.optimization_barrier(jnp.mean(centered * centered, -1, keepdims=True))
    return centered * lax.rsqrt(var + 1e-05)

def unit(value):
    return value * lax.rsqrt(lax.optimization_barrier(jnp.sum(value * value, -1, keepdims=True)) + 1e-06)

def time_bias(buckets, rab, dtype):
    nbuck = rab.shape[1]
    levels = jnp.arange(nbuck, dtype=jnp.int32)
    gapgrid = jnp.abs(levels[:, None] - levels[None, :])
    gap_hot = (gapgrid[:, :, None] == levels[None, None, :]).astype(dtype)
    pair_bias = jnp.einsum('nmd,hd->hnm', gap_hot, rab, precision=HIGH)
    token_hot = (buckets[:, None] == levels[None, :]).astype(dtype)
    left = jnp.einsum('in,hnm->him', token_hot, pair_bias, precision=HIGH)
    return jnp.einsum('him,jm->hij', left, token_hot, precision=HIGH)

def hstu(emb, buckets, segment, w_in, b_in, w_out, rab):
    count = emb.shape[0]
    heads = rab.shape[0]
    hidden = jax.nn.silu(jnp.dot(layer_norm(emb), w_in, precision=HIGH, preferred_element_type=jnp.float32) + b_in)
    upart, vpart, qpart, kpart = jnp.split(hidden, 4, axis=1)
    qpart = qpart.reshape(count, heads, -1)
    kpart = kpart.reshape(count, heads, -1)
    vpart = vpart.reshape(count, heads, -1)
    scores = jnp.einsum('ihd,jhd->hij', qpart, kpart, precision=HIGH) * qpart.shape[2] ** (-0.5)
    scores = scores + time_bias(buckets, rab, emb.dtype)
    places = jnp.arange(count, dtype=jnp.int32)
    allowed = (places[None, :] <= places[:, None]) & (segment[None, :] == segment[:, None])
    weights = jax.nn.silu(scores) * allowed.astype(emb.dtype) / MOST_LEN
    mixed = jnp.einsum('hij,jhd->ihd', weights, vpart, precision=HIGH).reshape(count, -1)
    return jnp.dot(layer_norm(mixed) * upart, w_out, precision=HIGH, preferred_element_type=jnp.float32) + emb

def segments_of(lengths, count):
    ends = jnp.cumsum(lengths)
    places = jnp.arange(count, dtype=jnp.int32)
    segment = lax.optimization_barrier(jnp.sum((places[:, None] >= ends[None, :]).astype(jnp.int32), 1))
    following = jnp.concatenate([segment[1:], jnp.full((1,), -1, segment.dtype)])
    valid = (following == segment).astype(jnp.float32)
    return (segment, valid)

def device_terms(emb, buckets, lengths, negatives, w_in, b_in, w_out, rab):
    segment, valid = segments_of(lengths, emb.shape[0])
    valid = valid.astype(emb.dtype)

    def loss_of(inputs):
        states = unit(hstu(inputs, buckets, segment, w_in, b_in, w_out, rab))
        target = jnp.concatenate([inputs[1:], jnp.zeros((1, inputs.shape[1]), inputs.dtype)])
        target = unit(target)
        positive = lax.optimization_barrier(jnp.sum(states * target, -1)) / TEMPER
        logits = jnp.dot(states, negatives.T, precision=HIGH, preferred_element_type=jnp.float32) / TEMPER
        total = jnp.exp(positive) + lax.optimization_barrier(jnp.sum(jnp.exp(logits), 1))
        loss = valid * (jnp.log(total) - positive)
        return (jnp.sum(loss), loss)
    primal, back, loss = jax.vjp(loss_of, emb, has_aux=True)
    grad = back(jnp.ones((), emb.dtype))[0]
    return (grad, loss)

def reference(item_ids, seq_lengths, time_buckets, neg_ids, table, w_in, b_in, w_out, rab):
    width = table.shape[1]
    devices = N_SHARD * N_GROUP
    emb = table[item_ids].reshape(devices, TOK_DEV, width)
    buckets = time_buckets.reshape(devices, TOK_DEV)
    negatives = unit(table[neg_ids])

    def one(index):
        shard_index = index // N_GROUP
        return device_terms(emb[index], buckets[index], seq_lengths[index], negatives[shard_index], w_in, b_in, w_out, rab)
    grads, losses = lax.map(one, jnp.arange(devices, dtype=jnp.int32))
    table_grad = jax.ops.segment_sum(grads.reshape(-1, width), item_ids, num_segments=ROWS_DEV * N_GROUP)
    return (table_grad, losses.reshape(-1))
```

```python
import functools

import jax
import jax.numpy as jnp
from jax import lax
from jax.experimental import pallas as pl
from jax.experimental.pallas import tpu as pltpu
from jax.sharding import PartitionSpec as P

MOST_LEN = 64


HIGH = lax.Precision.HIGH
TEMPER = 0.05
MESH = pl.DeviceIdType.MESH
F32 = jnp.float32
BF16 = jnp.bfloat16


def pieces_of(value, count):
    terms = []
    for _ in range(count):
        term = value.astype(BF16)
        terms.append(term)
        value = value - term.astype(F32)
    return terms


def select_dot(onehot, value, count=3):
    return sum(jnp.dot(onehot, term, preferred_element_type=F32) for term in pieces_of(value, count))


def iota(shape, dim):
    return lax.broadcasted_iota(jnp.int32, shape, dim)


def hot(mask):
    return mask.astype(F32).astype(BF16)


def greet(sem, device):
    pl.semaphore_signal(sem, inc=1, device_id=device, device_id_type=MESH)


def remote(src, dst, send_sem, recv_sem, device):
    return pltpu.make_async_remote_copy(
        src_ref=src, dst_ref=dst, send_sem=send_sem, recv_sem=recv_sem, device_id=device, device_id_type=MESH
    )


def rows8(index, rows=8):
    return pl.ds(pl.multiple_of(index * rows, rows), rows)


def fetch_kernel(
    dims, ids_ref, neg_ref, table_ref, emb_ref, panel_ref, place_ref, picks_ref,
    req_out, req_in, expand, served, recv, req_sems, row_sems, neg_send, neg_recv,
):
    nx, ny = dims
    groups = nx * ny * 2
    count = ids_ref.shape[1]
    nneg = neg_ref.shape[1]
    slots = groups * 8
    me = lax.axis_index("group")
    core = lax.rem(me, 2)
    x, y = me // (2 * ny), lax.rem(me // 2, ny)

    def at(xx, yy, cc):
        return (lax.rem(xx + nx, nx) * ny + lax.rem(yy + ny, ny)) * 2 + cc

    barrier = pltpu.get_barrier_semaphore()

    def hello(k, c):
        greet(barrier, {"group": lax.rem(me + k, groups)})
        return c

    lax.fori_loop(1, groups, hello, 0)

    ids = jnp.broadcast_to(ids_ref[...], (count, count))
    ids_t = ids.T
    rows_dev = table_ref.shape[0]
    own_row, own_col = ids // rows_dev, ids_t // rows_dev
    same = own_row == own_col
    col, row = iota((count, count), 1), iota((count, count), 0)
    rank_col = jnp.sum(jnp.where(same & (col < row), 1, 0), axis=1, keepdims=True)
    rank_row = jnp.sum(jnp.where(same & (row < col), 1, 0), axis=0, keepdims=True)
    slot_col = own_col[:, :1] * 8 + rank_col
    slot_row = own_row[:1] * 8 + rank_row
    owner_hot = hot(jnp.broadcast_to(own_row[:1], (groups, count)) == iota((groups, count), 0))
    wanted = jnp.where(lax.rem(col, 4) == rank_col, ids_t - own_col * rows_dev + 1, 0)
    requests = jnp.dot(owner_hot, wanted.astype(F32).astype(BF16), preferred_element_type=F32)
    for g in range(groups):
        req_out[g] = requests[g : g + 1].astype(jnp.int32)
    neg_row = lax.rem(neg_ref[...], rows_dev)
    neg_hot = hot(jnp.broadcast_to(neg_row, (rows_dev, nneg)) == iota((rows_dev, nneg), 0)).T
    drawn = select_dot(neg_hot, table_ref[...])
    mine = rows8(me, nneg)
    panel_ref[mine] = drawn * lax.rsqrt(jnp.sum(drawn * drawn, -1, keepdims=True) + 1e-06)
    pl.semaphore_wait(barrier, groups - 1)

    def ask(k, c):
        peer = lax.rem(me + k, groups)
        remote(req_out.at[peer], req_in.at[me], req_sems.at[0], req_sems.at[1], {"group": peer}).start()
        return c

    lax.fori_loop(1, groups, ask, 0)
    req_in[me] = req_out[me]

    def pass_on(block, device):
        where = rows8(block, nneg)
        remote(panel_ref.at[where], panel_ref.at[where], neg_send, neg_recv.at[block], {"group": device}).start()

    def arrive(block):
        where = rows8(block, nneg)
        remote(panel_ref.at[where], panel_ref.at[where], neg_send, neg_recv.at[block], {"group": me}).wait_recv()

    sibling = at(x, y, 1 - core)

    def along_y(block, up, down):
        if up:
            pass_on(block, at(x, y + 1, core))
        if down:
            pass_on(block, at(x, y - 1, core))
        pass_on(block, at(x + 1, y, core))
        pass_on(block, at(x - 1, y, core))
        pass_on(block, sibling)

    ups, downs = ny // 2, (ny - 1) // 2
    along_y(me, True, True)

    def asked():
        return remote(
            req_out.at[pl.ds(0, groups - 1)], req_in.at[pl.ds(0, groups - 1)], req_sems.at[0], req_sems.at[1], {"group": me}
        )

    asked().wait_recv()

    def widen(g, c):
        expand[rows8(g)] = jnp.broadcast_to(req_in[g], (8, count))
        return c

    lax.fori_loop(0, groups, widen, 0)
    lanes, subs = iota((slots, count), 1), lax.rem(iota((slots, count), 0), 8)
    kept = jnp.where(lanes == lax.rem(subs, 4), expand[...], 0).astype(F32).astype(BF16)
    ones = jnp.ones((count, count), BF16)
    named = jnp.dot(kept, ones, preferred_element_type=F32).astype(jnp.int32)
    named_t = lax.dot_general(ones, kept, (((1,), (1,)), ((), ())), preferred_element_type=F32).astype(jnp.int32)
    fits = named == lanes + 1
    serve = jnp.concatenate([hot(fits & (subs < 4)), hot(fits & (subs >= 4))], axis=1)
    half = table_ref.shape[1] // 2
    stacked = jnp.concatenate([table_ref[:, :half], table_ref[:, half:]], axis=0)
    served[...] = select_dot(serve, stacked)

    def give(k, c):
        peer = lax.rem(me + k, groups)
        remote(served.at[rows8(peer)], recv.at[rows8(me)], row_sems.at[0], row_sems.at[1], {"group": peer}).start()
        return c

    lax.fori_loop(1, groups, give, 0)
    recv[rows8(me)] = served[rows8(me)]
    fits_t = named_t == iota((count, slots), 0) + 1
    subs_t = lax.rem(iota((count, slots), 1), 8)
    picks_ref[0] = hot(fits_t & (subs_t < 4))
    picks_ref[1] = hot(fits_t & (subs_t >= 4))
    slot_sub = iota((slots, count), 0)
    place_ref[:, :count] = hot(slot_sub == slot_row)
    place_ref[:, count:] = hot(slot_sub == slot_row + 4)

    for k in range(1, ups + 1):
        block = at(x, y - k, core)
        arrive(block)
        along_y(block, k < ups, False)
        if k <= downs:
            block = at(x, y + k, core)
            arrive(block)
            along_y(block, False, k < downs)
    order = [0] + [s * k for k in range(1, ups + 1) for s in (-1, 1) if s < 0 or k <= downs]
    for dy in order:
        for dx in (-1, 1):
            block = at(x + dx, y + dy, core)
            arrive(block)
            if (dy % 2 == 0) == (dx < 0):
                pass_on(block, at(x - dx, y, core))
            pass_on(block, sibling)
    for dy in order:
        block = at(x + 2, y + dy, core)
        arrive(block)
        pass_on(block, sibling)

    def given():
        return remote(
            served.at[pl.ds(0, (groups - 1) * 8)], recv.at[pl.ds(0, (groups - 1) * 8)], row_sems.at[0], row_sems.at[1],
            {"group": me},
        )

    given().wait_recv()
    slot_lane = iota((count, slots), 1)
    for q in range(2):
        emb_ref[:, q * half : (q + 1) * half] = select_dot(hot(slot_lane == slot_col + 4 * q), recv[...])
    for dx in range(nx):
        for dy in range(ny):
            arrive(at(x + dx, y + dy, 1 - core))
    asked().wait_send()
    given().wait_send()
    sent = pl.ds(0, (groups - 1) * nneg)
    remote(panel_ref.at[sent], panel_ref.at[sent], neg_send, neg_recv.at[0], {"group": me}).wait_send()


def fetch(dims, ids, negs, table):
    groups = dims[0] * dims[1] * 2
    count, width, nneg = ids.shape[1], table.shape[1], negs.shape[1]
    slots = groups * 8
    vm = pl.BlockSpec(memory_space=pltpu.VMEM)
    shape = jax.ShapeDtypeStruct
    return pl.pallas_call(
        functools.partial(fetch_kernel, dims),
        out_shape=(
            shape((count, width), F32),
            shape((groups * nneg, width), F32),
            shape((slots, 2 * count), BF16),
            shape((2, count, slots), BF16),
        ),
        in_specs=[vm] * 3,
        out_specs=(vm,) * 4,
        scratch_shapes=[
            pltpu.VMEM((groups, 1, count), jnp.int32),
            pltpu.VMEM((groups, 1, count), jnp.int32),
            pltpu.VMEM((slots, count), jnp.int32),
            pltpu.VMEM((slots, width // 2), F32),
            pltpu.VMEM((slots, width // 2), F32),
            pltpu.SemaphoreType.DMA((2,)),
            pltpu.SemaphoreType.DMA((2,)),
            pltpu.SemaphoreType.DMA,
            pltpu.SemaphoreType.DMA((groups,)),
        ],
        compiler_params=pltpu.CompilerParams(collective_id=0, has_side_effects=True, vmem_limit_bytes=48 << 20),
        name="fetch",
    )(ids, negs, table)

def grad_kernel(
    G, S, piece, grad_ref, place_ref, pick_ref, red_ref, out_ref, recv, part, rs, send_sem, recv_sem, rs_send, rs_recv, ag_send, ag_recv,
):
    me = lax.axis_index("group")
    my = lax.axis_index("shard")
    barrier = pltpu.get_barrier_semaphore()

    def greet(k, c):
        pl.semaphore_signal(barrier, inc=1, device_id={"group": lax.rem(me + k, G)}, device_id_type=MESH)
        return c

    lax.fori_loop(1, G, greet, 0)

    def greet_s(k, c):
        pl.semaphore_signal(barrier, inc=1, device_id={"shard": lax.rem(my + k, S)}, device_id_type=MESH)
        return c

    lax.fori_loop(1, S, greet_s, 0)
    chunks = out_ref.shape[0]
    for h in range(chunks):
        stacked = jnp.concatenate([grad_ref[:, (2 * h + q) * 128 : (2 * h + q + 1) * 128] for q in range(2)], axis=0)
        out_ref[h] = select_dot(place_ref[...], stacked)
    pl.semaphore_wait(barrier, G - 1 + S - 1)
    for h in range(chunks):

        def send(k, c):
            peer = lax.rem(me + k, G)
            pltpu.make_async_remote_copy(
                src_ref=out_ref.at[h, pl.ds(pl.multiple_of(peer * 8, 8), 8)],
                dst_ref=recv.at[h, pl.ds(pl.multiple_of(me * 8, 8), 8)],
                send_sem=send_sem.at[h],
                recv_sem=recv_sem.at[h],
                device_id={"group": peer},
                device_id_type=MESH,
            ).start()
            return c

        lax.fori_loop(1, G, send, 0)
        own = pl.ds(pl.multiple_of(me * 8, 8), 8)
        recv[h, own] = out_ref[h, own]

    def whole(h):
        return pltpu.make_async_remote_copy(
            src_ref=out_ref.at[h, pl.ds(0, (G - 1) * 8)],
            dst_ref=recv.at[h, pl.ds(0, (G - 1) * 8)],
            send_sem=send_sem.at[h],
            recv_sem=recv_sem.at[h],
            device_id={"group": me},
            device_id_type=MESH,
        )

    half = 256
    for h in range(chunks):
        whole(h).wait_recv()
        part[h, pl.ds(half, part.shape[1] - half)] = jnp.zeros((part.shape[1] - half, 128), F32)
        for q in range(2):
            part[h, pl.ds(q * 128, 128)] = select_dot(pick_ref[q], recv[h])

        def scatter(k, c):
            peer = lax.rem(my + k, S)
            pltpu.make_async_remote_copy(
                src_ref=part.at[h, pl.ds(pl.multiple_of(peer * piece, 8), piece)],
                dst_ref=rs.at[h, my],
                send_sem=rs_send.at[h],
                recv_sem=rs_recv.at[h],
                device_id={"shard": peer},
                device_id_type=MESH,
            ).start()
            return c

        lax.fori_loop(1, S, scatter, 0)
        rs[h, my] = part[h, pl.ds(pl.multiple_of(my * piece, 8), piece)]

    def whole_rs(h):
        return pltpu.make_async_remote_copy(
            src_ref=rs.at[h, pl.ds(0, S - 1)],
            dst_ref=rs.at[h, pl.ds(0, S - 1)],
            send_sem=rs_send.at[h],
            recv_sem=rs_recv.at[h],
            device_id={"shard": my},
            device_id_type=MESH,
        )

    mine = pl.ds(pl.multiple_of(my * piece, 8), piece)
    for h in range(chunks):
        whole_rs(h).wait_recv()
        red_ref[h, mine] = jnp.sum(rs[h], axis=0)

        def spread(k, c):
            peer = lax.rem(my + k, S)
            pltpu.make_async_remote_copy(
                src_ref=red_ref.at[h, mine],
                dst_ref=red_ref.at[h, mine],
                send_sem=ag_send.at[h],
                recv_sem=ag_recv.at[h],
                device_id={"shard": peer},
                device_id_type=MESH,
            ).start()
            return c

        lax.fori_loop(1, S, spread, 0)
    for h in range(chunks):
        tail = pltpu.make_async_remote_copy(
            src_ref=red_ref.at[h, pl.ds(0, (S - 1) * piece)],
            dst_ref=red_ref.at[h, pl.ds(0, (S - 1) * piece)],
            send_sem=ag_send.at[h],
            recv_sem=ag_recv.at[h],
            device_id={"shard": my},
            device_id_type=MESH,
        )
        tail.wait_recv()
        tail.wait_send()
        whole(h).wait_send()
        whole_rs(h).wait_send()


def exchange_grads(grads, place, picks, G, S):
    count, width = grads.shape
    chunks, slots = width // 256, place.shape[0]
    piece = (-(-256 // S) + 7) // 8 * 8
    rows = S * piece
    vm = pl.BlockSpec(memory_space=pltpu.VMEM)
    red = pl.pallas_call(
        functools.partial(grad_kernel, G, S, piece),
        out_shape=jax.ShapeDtypeStruct((chunks, rows, 128), F32),
        in_specs=[vm] * 3,
        out_specs=vm,
        scratch_shapes=[
            pltpu.VMEM((chunks, slots, 128), F32),
            pltpu.VMEM((chunks, slots, 128), F32),
            pltpu.VMEM((chunks, rows, 128), F32),
            pltpu.VMEM((chunks, S, piece, 128), F32),
        ]
        + [pltpu.SemaphoreType.DMA((chunks,))] * 6,
        compiler_params=pltpu.CompilerParams(collective_id=1, has_side_effects=True, vmem_limit_bytes=48 << 20),
        name="grad_exchange",
    )(grads, place, picks)
    parts = red[:, :256].reshape(chunks * 2, count, 128)
    return parts.transpose(1, 0, 2).reshape(count, width)

def layer_norm(value):
    mean = jnp.mean(value, -1, keepdims=True)
    centered = value - mean
    var = jnp.mean(centered * centered, -1, keepdims=True)
    return centered * lax.rsqrt(var + 1e-05)


def unit(value):
    return value * lax.rsqrt(jnp.sum(value * value, -1, keepdims=True) + 1e-06)


def time_bias(buckets, rab):
    nbuck = rab.shape[1]
    levels = jnp.arange(nbuck, dtype=jnp.int32)
    gapgrid = jnp.abs(levels[:, None] - levels[None, :])
    gap_hot = (gapgrid[:, :, None] == levels[None, None, :]).astype(jnp.float32)
    pair_bias = jnp.einsum("nmd,hd->hnm", gap_hot, rab, precision=HIGH)
    token_hot = (buckets[:, None] == levels[None, :]).astype(jnp.float32)
    left = jnp.einsum("in,hnm->him", token_hot, pair_bias, precision=HIGH)
    return jnp.einsum("him,jm->hij", left, token_hot, precision=HIGH)


def hstu(emb, buckets, segment, w_in, b_in, w_out, rab):
    count = emb.shape[0]
    heads = rab.shape[0]
    hidden = jax.nn.silu(
        jnp.dot(layer_norm(emb), w_in, precision=HIGH, preferred_element_type=jnp.float32) + b_in
    )
    upart, vpart, qpart, kpart = jnp.split(hidden, 4, axis=1)
    qpart = qpart.reshape(count, heads, -1)
    kpart = kpart.reshape(count, heads, -1)
    vpart = vpart.reshape(count, heads, -1)
    scores = jnp.einsum("ihd,jhd->hij", qpart, kpart, precision=HIGH) * qpart.shape[2] ** (-0.5)
    scores = scores + time_bias(buckets, rab)
    places = jnp.arange(count, dtype=jnp.int32)
    allowed = (places[None, :] <= places[:, None]) & (segment[None, :] == segment[:, None])
    weights = jax.nn.silu(scores) * allowed.astype(jnp.float32) / MOST_LEN
    mixed = jnp.einsum("hij,jhd->ihd", weights, vpart, precision=HIGH).reshape(count, -1)
    return (
        jnp.dot(
            layer_norm(mixed) * upart, w_out, precision=HIGH, preferred_element_type=jnp.float32
        )
        + emb
    )


def body(item_ids, seq_lengths, time_buckets, neg_ids, table, w_in, b_in, w_out, rab):
    groups, shards = lax.axis_size("group"), lax.axis_size("shard")
    width = table.shape[1]
    count = item_ids.shape[0]
    emb, panel_rows, place, picks = fetch((groups // 16, 8), item_ids.reshape(1, -1), neg_ids, table)
    lengths = seq_lengths.reshape(-1)
    ends = jnp.cumsum(lengths)
    places = jnp.arange(count, dtype=jnp.int32)
    segment = jnp.sum((places[:, None] >= ends[None, :]).astype(jnp.int32), 1)
    following = jnp.concatenate([segment[1:], jnp.full((1,), -1, jnp.int32)])
    valid = (following == segment).astype(jnp.float32)

    def states_of(inputs):
        states = unit(hstu(inputs, time_buckets, segment, w_in, b_in, w_out, rab))
        shifted = jnp.concatenate([inputs[1:], jnp.zeros((1, width), jnp.float32)])
        return (states, unit(shifted))

    (states, target), back = jax.vjp(states_of, emb)
    exps = jnp.exp(
        jnp.dot(states, panel_rows.T, precision=HIGH, preferred_element_type=jnp.float32) / TEMPER
    )
    zneg = jnp.sum(exps, 1)
    pulled = jnp.dot(exps, panel_rows, precision=HIGH, preferred_element_type=jnp.float32)
    positive = jnp.sum(states * target, -1) / TEMPER
    expos = jnp.exp(positive)
    total = expos + zneg
    token_loss = valid * (jnp.log(total) - positive)
    share = expos / total - 1.0
    d_states = valid[:, None] * (share[:, None] * target + pulled / total[:, None]) / TEMPER
    d_target = valid[:, None] * (share[:, None] * states) / TEMPER
    d_emb = back((d_states, d_target))[0]
    table_grad = exchange_grads(d_emb, place, picks, groups, shards)
    return (table_grad, token_loss)


def solution(mesh):
    in_specs = (
        P(("shard", "group")),
        P(("shard", "group"), None),
        P(("shard", "group")),
        P("shard", "group"),
        P("group", None),
        P(),
        P(),
        P(),
        P(),
    )
    out_specs = (P("group", None), P(("shard", "group")))
    return jax.shard_map(body, mesh=mesh, in_specs=in_specs, out_specs=out_specs, check_vma=False)
```

```python
import functools

import jax
import jax.numpy as jnp
from jax import lax
from jax.experimental import pallas as pl
from jax.experimental.pallas import tpu as pltpu
from jax.sharding import PartitionSpec as P

MOST_LEN = 64
TEMPER = 0.05
MESH = pl.DeviceIdType.MESH
F32 = jnp.float32
BF16 = jnp.bfloat16


def pieces_of(value, count):
    terms = []
    for _ in range(count):
        term = value.astype(BF16)
        terms.append(term)
        value = value - term.astype(F32)
    return terms


def select_dot(onehot, value, count=3):
    return sum(jnp.dot(onehot, term, preferred_element_type=F32) for term in pieces_of(value, count))


def iota(shape, dim):
    return lax.broadcasted_iota(jnp.int32, shape, dim)


def hot(mask):
    return mask.astype(F32).astype(BF16)


def greet(sem, device):
    pl.semaphore_signal(sem, inc=1, device_id=device, device_id_type=MESH)


def remote(src, dst, send_sem, recv_sem, device):
    return pltpu.make_async_remote_copy(
        src_ref=src, dst_ref=dst, send_sem=send_sem, recv_sem=recv_sem, device_id=device, device_id_type=MESH
    )


def rows8(index, rows=8):
    return pl.ds(pl.multiple_of(index * rows, rows), rows)


def weights_of(value):
    high = value.astype(BF16)
    return high, (value - high.astype(F32)).astype(BF16)


NN = (((1,), (0,)), ((), ()))
NT = (((1,), (1,)), ((), ()))


def mul3(left, high, low, dims=NN):
    count = left.shape[0]
    lhigh, llow = weights_of(left)
    both = lax.dot_general(jnp.concatenate([lhigh, llow], axis=0), high, dims, preferred_element_type=F32)
    return both[:count] + both[count:] + lax.dot_general(lhigh, low, dims, preferred_element_type=F32)


def rows_sum(value):
    return jnp.sum(value, axis=-1, keepdims=True)


def norm_back(d_norm, norm, scale):
    width = norm.shape[-1]
    return scale * (d_norm - rows_sum(d_norm) / width - norm * (rows_sum(d_norm * norm) / width))


def step_kernel(
    dims, shards, piece, heads,
    ids_h, len_h, time_h, neg_h, table_h, w_in_h, b_in_h, w_out_h, rab_h,
    red_ref, loss_ref,
    ids_v, len_s, time_v, neg_v, table_v, w_in_v, b_in_v, w_out_v, rab_s, load_sems,
    in_hi, in_lo, out_hi, out_lo, panel,
    req_out, req_in, expand, served, recv, place, picks,
    emb, norm, hid, slope, gap, bias, attn, attn_slope, mixed, dhid,
    outgoing, incoming, part, rsum,
    req_sems, row_sems, neg_send, neg_recv, send_sem, recv_sem, rs_send, rs_recv, ag_send, ag_recv,
):
    nx, ny = dims
    groups = nx * ny * 2
    count = ids_v.shape[1]
    width = table_v.shape[1]
    nneg = neg_v.shape[1]
    slots = groups * 8
    me, my = lax.axis_index("group"), lax.axis_index("shard")
    core = lax.rem(me, 2)
    x, y = me // (2 * ny), lax.rem(me // 2, ny)

    def at(xx, yy, cc):
        return (lax.rem(xx + nx, nx) * ny + lax.rem(yy + ny, ny)) * 2 + cc

    barrier = pltpu.get_barrier_semaphore()
    pairs = [
        (ids_h, ids_v), (table_h, table_v), (neg_h, neg_v), (len_h, len_s), (time_h, time_v), (rab_h, rab_s),
        (w_in_h, w_in_v), (w_out_h, w_out_v), (b_in_h, b_in_v),
    ]
    loads = [pltpu.make_async_copy(a, b, load_sems.at[i]) for i, (a, b) in enumerate(pairs)]
    for load in loads:
        load.start()

    def hello(k, c):
        greet(barrier, {"group": lax.rem(me + k, groups)})
        return c

    lax.fori_loop(1, groups, hello, 0)

    def hello_z(k, c):
        greet(barrier, {"shard": lax.rem(my + k, shards)})
        return c

    lax.fori_loop(1, shards, hello_z, 0)
    loads[0].wait()
    ids = jnp.broadcast_to(ids_v[...], (count, count))
    ids_t = ids.T
    rows_dev = table_v.shape[0]
    own_row, own_col = ids // rows_dev, ids_t // rows_dev
    same = own_row == own_col
    col, row = iota((count, count), 1), iota((count, count), 0)
    rank_col = jnp.sum(jnp.where(same & (col < row), 1, 0), axis=1, keepdims=True)
    rank_row = jnp.sum(jnp.where(same & (row < col), 1, 0), axis=0, keepdims=True)
    slot_col = own_col[:, :1] * 8 + rank_col
    slot_row = own_row[:1] * 8 + rank_row
    owner_hot = hot(jnp.broadcast_to(own_row[:1], (groups, count)) == iota((groups, count), 0))
    wanted = jnp.where(lax.rem(col, 4) == rank_col, ids_t - own_col * rows_dev + 1, 0)
    requests = jnp.dot(owner_hot, wanted.astype(F32).astype(BF16), preferred_element_type=F32)
    for g in range(groups):
        req_out[g] = requests[g : g + 1].astype(jnp.int32)
    loads[1].wait()
    loads[2].wait()
    pl.semaphore_wait(barrier, groups - 1 + shards - 1)

    def ask(k, c):
        peer = lax.rem(me + k, groups)
        remote(req_out.at[peer], req_in.at[me], req_sems.at[0], req_sems.at[1], {"group": peer}).start()
        return c

    lax.fori_loop(1, groups, ask, 0)
    req_in[me] = req_out[me]
    neg_row = lax.rem(neg_v[...], rows_dev)
    neg_hot = hot(jnp.broadcast_to(neg_row, (rows_dev, nneg)) == iota((rows_dev, nneg), 0)).T
    drawn = select_dot(neg_hot, table_v[...])
    mine = rows8(me, nneg)
    panel[mine] = drawn * lax.rsqrt(rows_sum(drawn * drawn) + 1e-06)

    def pass_on(block, device):
        where = rows8(block, nneg)
        remote(panel.at[where], panel.at[where], neg_send, neg_recv.at[block], {"group": device}).start()

    def arrive(block):
        where = rows8(block, nneg)
        remote(panel.at[where], panel.at[where], neg_send, neg_recv.at[block], {"group": me}).wait_recv()

    sibling = at(x, y, 1 - core)

    def along_y(block, up, down):
        if up:
            pass_on(block, at(x, y + 1, core))
        if down:
            pass_on(block, at(x, y - 1, core))
        pass_on(block, at(x + 1, y, core))
        pass_on(block, at(x - 1, y, core))
        pass_on(block, sibling)

    ups, downs = ny // 2, (ny - 1) // 2
    along_y(me, True, True)

    def asked():
        return remote(
            req_out.at[pl.ds(0, groups - 1)], req_in.at[pl.ds(0, groups - 1)], req_sems.at[0], req_sems.at[1], {"group": me}
        )

    asked().wait_recv()

    def widen(g, c):
        expand[rows8(g)] = jnp.broadcast_to(req_in[g], (8, count))
        return c

    lax.fori_loop(0, groups, widen, 0)
    lanes, subs = iota((slots, count), 1), lax.rem(iota((slots, count), 0), 8)
    kept = jnp.where(lanes == lax.rem(subs, 4), expand[...], 0).astype(F32).astype(BF16)
    ones = jnp.ones((count, count), BF16)
    named = jnp.dot(kept, ones, preferred_element_type=F32).astype(jnp.int32)
    fits = named == lanes + 1
    serve = jnp.concatenate([hot(fits & (subs < 4)), hot(fits & (subs >= 4))], axis=1)
    half = width // 2
    stacked = jnp.concatenate([table_v[:, :half], table_v[:, half:]], axis=0)
    served[...] = select_dot(serve, stacked)

    def give(k, c):
        peer = lax.rem(me + k, groups)
        remote(served.at[rows8(peer)], recv.at[rows8(me)], row_sems.at[0], row_sems.at[1], {"group": peer}).start()
        return c

    lax.fori_loop(1, groups, give, 0)
    recv[rows8(me)] = served[rows8(me)]
    for k in range(1, ups + 1):
        block = at(x, y - k, core)
        arrive(block)
        along_y(block, k < ups, False)
        if k <= downs:
            block = at(x, y + k, core)
            arrive(block)
            along_y(block, False, k < downs)
    named_t = lax.dot_general(ones, kept, NT, preferred_element_type=F32).astype(jnp.int32)
    fits_t = named_t == iota((count, slots), 0) + 1
    subs_t = lax.rem(iota((count, slots), 1), 8)
    picks[0] = hot(fits_t & (subs_t < 4))
    picks[1] = hot(fits_t & (subs_t >= 4))
    slot_sub = iota((slots, count), 0)
    place[:, :count] = hot(slot_sub == slot_row)
    place[:, count:] = hot(slot_sub == slot_row + 4)
    for load in loads[3:]:
        load.wait()

    def refine(source, high, low):
        def body(i, c):
            where = rows8(i, 32)
            high[where], low[where] = weights_of(source[where])
            return c

        lax.fori_loop(0, width // 32, body, 0)

    refine(w_in_v, in_hi, in_lo)
    refine(w_out_v, out_hi, out_lo)
    times = jnp.broadcast_to(time_v[...], (count, count))
    gap[...] = jnp.abs(times - times.T)
    buckets = rab_s.shape[1]
    for b in range(4):
        where = slice(b * count // 4, (b + 1) * count // 4)
        gaps = gap[where]

        def look(d, sums):
            for e in range(4):
                here = gaps == d * 4 + e
                sums = tuple(jnp.where(here, rab_s[n, d * 4 + e], s) for n, s in enumerate(sums))
            return sums

        found = lax.fori_loop(0, buckets // 4, look, (jnp.zeros(gaps.shape, F32),) * heads)
        for n in range(heads):
            bias[n, where] = found[n]
    seg_row, seg_col = jnp.zeros((count, count), jnp.int32), jnp.zeros((count, count), jnp.int32)
    place_col = iota((count, 1), 0)
    valid = jnp.ones((count, 1), F32)
    end = 0
    for s in range(len_s.shape[1]):
        end = end + len_s[0, s]
        seg_row += jnp.where(col >= end, 1, 0)
        seg_col += jnp.where(row >= end, 1, 0)
        valid = jnp.where(place_col + 1 == end, 0.0, valid)
    allowed = jnp.where((col <= row) & (seg_row == seg_col), 1.0 / MOST_LEN, 0.0)
    valid = jnp.where(place_col + 1 == count, 0.0, valid)

    def given():
        return remote(
            served.at[pl.ds(0, (groups - 1) * 8)], recv.at[pl.ds(0, (groups - 1) * 8)], row_sems.at[0], row_sems.at[1],
            {"group": me},
        )

    given().wait_recv()
    slot_lane = iota((count, slots), 1)
    for q in range(2):
        emb[:, q * half : (q + 1) * half] = select_dot(hot(slot_lane == slot_col + 4 * q), recv[...])
    e = emb[...]
    e = e - rows_sum(e) / width
    scale1 = lax.rsqrt(rows_sum(e * e) / width + 1e-05)
    norm[...] = e * scale1
    for c in range(4):
        part_c = slice(c * width, (c + 1) * width)
        pre = mul3(norm[...], in_hi[:, part_c], in_lo[:, part_c]) + b_in_v[:, part_c]
        sig = 1.0 / (1.0 + jnp.exp(-pre))
        hid[:, part_c] = pre * sig
        slope[:, part_c] = sig * (1.0 + pre * (1.0 - sig))
    order = [0] + [s * k for k in range(1, ups + 1) for s in (-1, 1) if s < 0 or k <= downs]
    for dy in order:
        for dx in (-1, 1):
            block = at(x + dx, y + dy, core)
            arrive(block)
            if (dy % 2 == 0) == (dx < 0):
                pass_on(block, at(x - dx, y, core))
            pass_on(block, sibling)
    size = width // heads
    root = size ** (-0.5)

    def head(part_c, n):
        return slice(part_c * width + n * size, part_c * width + (n + 1) * size)

    for n in range(heads):
        score = mul3(hid[:, head(2, n)], *weights_of(hid[:, head(3, n)]), NT) * root + bias[n]
        sig = 1.0 / (1.0 + jnp.exp(-score))
        weight = score * sig * allowed
        attn[n] = weight
        attn_slope[n] = sig * (1.0 + score * (1.0 - sig)) * allowed
        mixed[:, head(0, n)] = mul3(weight, *weights_of(hid[:, head(1, n)]))
    for dy in order:
        block = at(x + 2, y + dy, core)
        arrive(block)
        pass_on(block, sibling)
    m = mixed[...]
    m = m - rows_sum(m) / width
    scale2 = lax.rsqrt(rows_sum(m * m) / width + 1e-05)
    mixed[...] = m * scale2
    out = mul3(mixed[...] * hid[:, :width], out_hi[...], out_lo[...]) + emb[...]
    scale3 = lax.rsqrt(rows_sum(out * out) + 1e-06)
    state = out * scale3
    e = emb[...]
    row_col = iota((count, width), 0)
    after = jnp.where(row_col == count - 1, 0.0, pltpu.roll(e, count - 1, 0))
    scale4 = lax.rsqrt(rows_sum(after * after) + 1e-06)
    target = after * scale4
    positive = rows_sum(state * target) / TEMPER
    zneg = jnp.zeros((count, 1), F32)
    pulled = jnp.zeros((count, width), F32)
    state_hi, state_lo = weights_of(state)
    state_two = jnp.concatenate([state_hi, state_lo], axis=0)
    for dx in (0, -1, 1, 2):
        for dy in range(ny):
            arrive(at(x + dx, y + dy, 1 - core))
        block = panel[rows8(lax.rem(x + dx + nx, nx), 2 * ny * nneg)]
        high, low = weights_of(block)
        logit = lax.dot_general(state_two, high, NT, preferred_element_type=F32)
        logit = logit[:count] + logit[count:] + lax.dot_general(state_hi, low, NT, preferred_element_type=F32)
        exps = jnp.exp(logit / TEMPER)
        zneg += rows_sum(exps)
        pulled += mul3(exps, high, low)
    expos = jnp.exp(positive)
    total = expos + zneg
    loss = valid * (jnp.log(total) - positive)
    loss_ref[...] = jnp.broadcast_to(loss, (count, count)).T[:1]
    share = expos / total - 1.0
    weigh = valid / TEMPER
    d_state = weigh * (share * target + pulled / total)
    d_target = (weigh * share) * state
    d_out = scale3 * (d_state - state * rows_sum(state * d_state))
    d_after = scale4 * (d_target - target * rows_sum(target * d_target))
    d_emb = d_out + jnp.where(row_col == 0, 0.0, pltpu.roll(d_after, 1, 0))
    emb[...] = d_emb
    d_gated = mul3(d_out, out_hi[...], out_lo[...], NT)
    dhid[:, :width] = d_gated * mixed[...] * slope[:, :width]
    mixed[...] = norm_back(d_gated * hid[:, :width], mixed[...], scale2)
    for n in range(heads):
        d_mix = mixed[:, head(0, n)]
        weight = attn[n]
        d_weight = mul3(d_mix, *weights_of(hid[:, head(1, n)]), NT)
        d_score = d_weight * attn_slope[n] * root
        mix_hi, mix_lo = weights_of(d_mix)
        dhid[:, head(1, n)] = mul3(weight.T, mix_hi, mix_lo) * slope[:, head(1, n)]
        dhid[:, head(2, n)] = mul3(d_score, *weights_of(hid[:, head(3, n)])) * slope[:, head(2, n)]
        dhid[:, head(3, n)] = mul3(d_score.T, *weights_of(hid[:, head(2, n)])) * slope[:, head(3, n)]
    d_norm = mul3(dhid[:, :width], in_hi[:, :width], in_lo[:, :width], NT)
    for c in range(1, 4):
        part_c = slice(c * width, (c + 1) * width)
        d_norm += mul3(dhid[:, part_c], in_hi[:, part_c], in_lo[:, part_c], NT)
    emb[...] += norm_back(d_norm, norm[...], scale1)
    chunks = outgoing.shape[0]
    for h in range(chunks):
        cols = [slice((2 * h + q) * 128, (2 * h + q + 1) * 128) for q in range(2)]
        outgoing[h] = select_dot(place[...], jnp.concatenate([emb[:, c] for c in cols], axis=0))

        def send(k, c):
            peer = lax.rem(me + k, groups)
            remote(
                outgoing.at[h, rows8(peer)], incoming.at[h, rows8(me)], send_sem.at[h], recv_sem.at[h], {"group": peer}
            ).start()
            return c

        lax.fori_loop(1, groups, send, 0)
        incoming[h, rows8(me)] = outgoing[h, rows8(me)]

    def whole(h):
        where = pl.ds(0, (groups - 1) * 8)
        return remote(outgoing.at[h, where], incoming.at[h, where], send_sem.at[h], recv_sem.at[h], {"group": me})

    for h in range(chunks):
        whole(h).wait_recv()
        spare = part.shape[1] - 2 * 128
        part[h, pl.ds(2 * 128, spare)] = jnp.zeros((spare, 128), F32)
        for q in range(2):
            part[h, pl.ds(q * 128, 128)] = select_dot(picks[q], incoming[h])

        def scatter(k, c):
            peer = lax.rem(my + k, shards)
            remote(part.at[h, rows8(peer, piece)], rsum.at[h, my], rs_send.at[h], rs_recv.at[h], {"shard": peer}).start()
            return c

        lax.fori_loop(1, shards, scatter, 0)
        rsum[h, my] = part[h, rows8(my, piece)]

    def whole_rs(h):
        where = pl.ds(0, shards - 1)
        return remote(rsum.at[h, where], rsum.at[h, where], rs_send.at[h], rs_recv.at[h], {"shard": my})

    own = rows8(my, piece)
    for h in range(chunks):
        whole_rs(h).wait_recv()
        red_ref[h, own] = jnp.sum(rsum[h], axis=0)

        def spread(k, c):
            peer = lax.rem(my + k, shards)
            remote(red_ref.at[h, own], red_ref.at[h, own], ag_send.at[h], ag_recv.at[h], {"shard": peer}).start()
            return c

        lax.fori_loop(1, shards, spread, 0)
    for h in range(chunks):
        where = pl.ds(0, (shards - 1) * piece)
        tail = remote(red_ref.at[h, where], red_ref.at[h, where], ag_send.at[h], ag_recv.at[h], {"shard": my})
        tail.wait_recv()
        tail.wait_send()
        whole(h).wait_send()
        whole_rs(h).wait_send()
    asked().wait_send()
    given().wait_send()
    sent = pl.ds(0, (groups - 1) * nneg)
    remote(panel.at[sent], panel.at[sent], neg_send, neg_recv.at[0], {"group": me}).wait_send()


def body(item_ids, seq_lengths, time_buckets, neg_ids, table, w_in, b_in, w_out, rab):
    groups, shards = lax.axis_size("group"), lax.axis_size("shard")
    count, width = item_ids.shape[0], table.shape[1]
    heads, hidden = rab.shape[0], w_in.shape[1]
    nneg = neg_ids.shape[1]
    slots, chunks = groups * 8, width // 256
    piece = (-(-256 // shards) + 7) // 8 * 8
    red_rows = shards * piece
    vm, smem, dma, i32 = pltpu.VMEM, pltpu.SMEM, pltpu.SemaphoreType.DMA, jnp.int32
    anywhere = pl.BlockSpec(memory_space=pl.ANY)
    red, loss = pl.pallas_call(
        functools.partial(step_kernel, (groups // 16, 8), shards, piece, heads),
        out_shape=(
            jax.ShapeDtypeStruct((chunks, red_rows, 128), F32),
            jax.ShapeDtypeStruct((1, count), F32),
        ),
        in_specs=[anywhere] * 9,
        out_specs=(pl.BlockSpec(memory_space=vm),) * 2,
        scratch_shapes=[
            vm((1, count), i32),
            smem(seq_lengths.shape, i32),
            vm((1, count), i32),
            vm((1, nneg), i32),
            vm(table.shape, F32),
            vm(w_in.shape, F32),
            vm((1, hidden), F32),
            vm(w_out.shape, F32),
            smem(rab.shape, F32),
            dma((9,)),
            vm(w_in.shape, BF16),
            vm(w_in.shape, BF16),
            vm(w_out.shape, BF16),
            vm(w_out.shape, BF16),
            vm((groups * nneg, width), F32),
            vm((groups, 1, count), i32),
            vm((groups, 1, count), i32),
            vm((slots, count), i32),
            vm((slots, width // 2), F32),
            vm((slots, width // 2), F32),
            vm((slots, 2 * count), BF16),
            vm((2, count, slots), BF16),
            vm((count, width), F32),
            vm((count, width), F32),
            vm((count, hidden), F32),
            vm((count, hidden), F32),
            vm((count, count), i32),
            vm((heads, count, count), F32),
            vm((heads, count, count), F32),
            vm((heads, count, count), F32),
            vm((count, width), F32),
            vm((count, hidden), F32),
            vm((chunks, slots, 128), F32),
            vm((chunks, slots, 128), F32),
            vm((chunks, red_rows, 128), F32),
            vm((chunks, shards, piece, 128), F32),
            dma((2,)),
            dma((2,)),
            dma,
            dma((groups,)),
        ]
        + [dma((chunks,))] * 6,
        compiler_params=pltpu.CompilerParams(collective_id=0, has_side_effects=True, vmem_limit_bytes=56 << 20),
        name="hstu_step",
    )(
        item_ids.reshape(1, -1), seq_lengths, time_buckets.reshape(1, -1), neg_ids, table, w_in, b_in.reshape(1, -1), w_out,
        rab,
    )
    parts = red[:, :256].reshape(chunks * 2, count, 128)
    return parts.transpose(1, 0, 2).reshape(count, width), loss.reshape(-1)


def solution(mesh):
    in_specs = (
        P(("shard", "group")),
        P(("shard", "group"), None),
        P(("shard", "group")),
        P("shard", "group"),
        P("group", None),
        P(),
        P(),
        P(),
        P(),
    )
    out_specs = (P("group", None), P(("shard", "group")))
    return jax.shard_map(body, mesh=mesh, in_specs=in_specs, out_specs=out_specs, check_vma=False)
```

```python
import functools

import jax
import jax.numpy as jnp
from jax import lax
from jax.experimental import pallas as pl
from jax.experimental.pallas import tpu as pltpu
from jax.sharding import PartitionSpec as P

MOST_LEN = 64
TEMPER = 0.05
MESH = pl.DeviceIdType.MESH
F32 = jnp.float32
BF16 = jnp.bfloat16


def pieces_of(value, count):
    terms = []
    for _ in range(count):
        term = value.astype(BF16)
        terms.append(term)
        value = value - term.astype(F32)
    return terms


def select_dot(onehot, value, count=3):
    return sum(jnp.dot(onehot, term, preferred_element_type=F32) for term in pieces_of(value, count))


def iota(shape, dim):
    return lax.broadcasted_iota(jnp.int32, shape, dim)


def hot(mask):
    return mask.astype(F32).astype(BF16)


def greet(sem, device):
    pl.semaphore_signal(sem, inc=1, device_id=device, device_id_type=MESH)


def remote(src, dst, send_sem, recv_sem, device):
    return pltpu.make_async_remote_copy(
        src_ref=src, dst_ref=dst, send_sem=send_sem, recv_sem=recv_sem, device_id=device, device_id_type=MESH
    )


def rows8(index, rows=8):
    return pl.ds(pl.multiple_of(index * rows, rows), rows)


def weights_of(value):
    high = value.astype(BF16)
    return high, (value - high.astype(F32)).astype(BF16)


NN = (((1,), (0,)), ((), ()))
NT = (((1,), (1,)), ((), ()))


def mul3(left, high, low, dims=NN):
    count = left.shape[0]
    lhigh, llow = weights_of(left)
    both = lax.dot_general(jnp.concatenate([lhigh, llow], axis=0), high, dims, preferred_element_type=F32)
    return both[:count] + both[count:] + lax.dot_general(lhigh, low, dims, preferred_element_type=F32)


def rows_sum(value):
    return jnp.sum(value, axis=-1, keepdims=True)


def norm_back(d_norm, norm, scale):
    width = norm.shape[-1]
    return scale * (d_norm - rows_sum(d_norm) / width - norm * (rows_sum(d_norm * norm) / width))


def step_kernel(
    dims, shards, piece, heads,
    ids_h, len_h, time_h, neg_h, table_h, w_in_h, b_in_h, w_out_h, rab_h,
    red_ref, loss_ref,
    ids_v, len_s, time_v, neg_v, table_v, w_in_v, b_in_v, w_out_v, rab_s, load_sems,
    in_hi, in_lo, out_hi, out_lo, panel,
    ids_all, expand, served, recv, place, picks,
    emb, norm, hid, slope, gap, bias, attn, attn_slope, mixed, dhid,
    outgoing, incoming, part, rsum,
    id_sems, row_sems, neg_send, neg_recv, send_sem, recv_sem, rs_send, rs_recv, ag_send, ag_recv,
):
    nx, ny = dims
    groups = nx * ny * 2
    count = ids_v.shape[1]
    width = table_v.shape[1]
    nneg = neg_v.shape[1]
    slots = groups * 8
    me, my = lax.axis_index("group"), lax.axis_index("shard")
    core = lax.rem(me, 2)
    x, y = me // (2 * ny), lax.rem(me // 2, ny)

    def at(xx, yy, cc):
        return (lax.rem(xx + nx, nx) * ny + lax.rem(yy + ny, ny)) * 2 + cc

    barrier = pltpu.get_barrier_semaphore()
    pairs = [
        (ids_h, ids_v), (table_h, table_v), (neg_h, neg_v), (len_h, len_s), (time_h, time_v), (rab_h, rab_s),
        (w_in_h, w_in_v), (w_out_h, w_out_v), (b_in_h, b_in_v),
    ]
    loads = [pltpu.make_async_copy(a, b, load_sems.at[i]) for i, (a, b) in enumerate(pairs)]
    for load in loads:
        load.start()

    def hello(k, c):
        greet(barrier, {"group": lax.rem(me + k, groups)})
        return c

    lax.fori_loop(1, groups, hello, 0)

    def hello_z(k, c):
        greet(barrier, {"shard": lax.rem(my + k, shards)})
        return c

    lax.fori_loop(1, shards, hello_z, 0)
    loads[0].wait()
    rows_dev = table_v.shape[0]
    ids_all[me] = ids_v[...]
    pl.semaphore_wait(barrier, groups - 1 + shards - 1)

    def fold(i, n):
        return jnp.where(lax.rem(i, 2) == 1, n // 2 - (i + 1) // 2, n // 2 + i // 2)

    def nth_peer(k):
        return at(x + fold(lax.rem(k, 2 * nx) // 2, nx), y + fold(k // (2 * nx), ny), lax.rem(core + 1 - lax.rem(k, 2), 2))

    def tell(k, c):
        remote(ids_all.at[me], ids_all.at[me], id_sems.at[0], id_sems.at[1], {"group": nth_peer(k)}).start()
        return c

    lax.fori_loop(0, groups - 1, tell, 0)
    loads[1].wait()
    loads[2].wait()
    neg_row = lax.rem(neg_v[...], rows_dev)
    neg_hot = hot(jnp.broadcast_to(neg_row, (rows_dev, nneg)) == iota((rows_dev, nneg), 0)).T
    drawn = select_dot(neg_hot, table_v[...])
    mine = rows8(me, nneg)
    panel[mine] = drawn * lax.rsqrt(rows_sum(drawn * drawn) + 1e-06)

    def pass_on(block, device):
        where = rows8(block, nneg)
        remote(panel.at[where], panel.at[where], neg_send, neg_recv.at[block], {"group": device}).start()

    def arrive(block):
        where = rows8(block, nneg)
        remote(panel.at[where], panel.at[where], neg_send, neg_recv.at[block], {"group": me}).wait_recv()

    sibling = at(x, y, 1 - core)

    def across_x(block):
        pass_on(block, at(x + 1, y, core))
        pass_on(block, at(x - 1, y, core))

    pass_on(me, at(x, y + 1, core))
    pass_on(me, at(x, y - 1, core))

    def told():
        where = pl.ds(0, groups - 1)
        return remote(ids_all.at[where], ids_all.at[where], id_sems.at[0], id_sems.at[1], {"group": me})

    across_x(me)
    pass_on(me, sibling)
    ups, downs = ny // 2, (ny - 1) // 2

    def step_y(k):
        block = at(x, y - k, core)
        arrive(block)
        if k < ups:
            pass_on(block, at(x, y + 1, core))
        across_x(block)
        pass_on(block, sibling)
        if k <= downs:
            block = at(x, y + k, core)
            arrive(block)
            if k < downs:
                pass_on(block, at(x, y - 1, core))
            across_x(block)
            pass_on(block, sibling)

    step_y(1)
    told().wait_recv()

    def widen(g, c):
        expand[rows8(g)] = jnp.broadcast_to(ids_all[g], (8, count))
        return c

    lax.fori_loop(0, groups, widen, 0)
    col, row = iota((count, count), 1), iota((count, count), 0)
    lanes, subs = iota((slots, count), 1), lax.rem(iota((slots, count), 0), 8)
    asked = expand[...]
    here = asked // rows_dev == me
    earlier = hot(row < col)
    turn = jnp.dot(hot(here), earlier, preferred_element_type=F32).astype(jnp.int32)
    kept = jnp.where(here & (turn == lax.rem(subs, 4)), asked - me * rows_dev + 1, 0).astype(F32).astype(BF16)
    ones = jnp.ones((count, count), BF16)
    named = jnp.dot(kept, ones, preferred_element_type=F32).astype(jnp.int32)
    fits = named == lanes + 1
    serve = jnp.concatenate([hot(fits & (subs < 4)), hot(fits & (subs >= 4))], axis=1)
    half = width // 2
    stacked = jnp.concatenate([table_v[:, :half], table_v[:, half:]], axis=0)
    served[...] = select_dot(serve, stacked)

    def give(k, c):
        peer = nth_peer(k)
        remote(served.at[rows8(peer)], recv.at[rows8(me)], row_sems.at[0], row_sems.at[1], {"group": peer}).start()
        return c

    recv[rows8(me)] = served[rows8(me)]
    for k in range(2, ups + 1):
        lax.fori_loop((groups - 1) * (k - 2) // (ups - 1), (groups - 1) * (k - 1) // (ups - 1), give, 0)
        step_y(k)
    order = [0] + [s * k for k in range(1, ups + 1) for s in (-1, 1) if s < 0 or k <= downs]

    def step_x(dy):
        for dx in (-1, 1):
            block = at(x + dx, y + dy, core)
            arrive(block)
            if (dy % 2 == 0) == (dx < 0):
                pass_on(block, at(x - dx, y, core))
            pass_on(block, sibling)

    step_x(order[0])
    ids = jnp.broadcast_to(ids_v[...], (count, count))
    ids_t = ids.T
    own_row, own_col = ids // rows_dev, ids_t // rows_dev
    same = own_row == own_col
    rank_col = jnp.sum(jnp.where(same & (col < row), 1, 0), axis=1, keepdims=True)
    rank_row = jnp.sum(jnp.where(same & (row < col), 1, 0), axis=0, keepdims=True)
    slot_col = own_col[:, :1] * 8 + rank_col
    slot_row = own_row[:1] * 8 + rank_row
    named_t = lax.dot_general(ones, kept, NT, preferred_element_type=F32).astype(jnp.int32)
    fits_t = named_t == iota((count, slots), 0) + 1
    subs_t = lax.rem(iota((count, slots), 1), 8)
    picks[0] = hot(fits_t & (subs_t < 4))
    picks[1] = hot(fits_t & (subs_t >= 4))
    slot_sub = iota((slots, count), 0)
    place[:, :count] = hot(slot_sub == slot_row)
    place[:, count:] = hot(slot_sub == slot_row + 4)
    for load in loads[3:]:
        load.wait()
    step_x(order[1])

    def refine(source, high, low):
        def body(i, c):
            where = rows8(i, 32)
            high[where], low[where] = weights_of(source[where])
            return c

        lax.fori_loop(0, width // 32, body, 0)

    refine(w_in_v, in_hi, in_lo)
    step_x(order[2])
    refine(w_out_v, out_hi, out_lo)
    times = jnp.broadcast_to(time_v[...], (count, count))
    gap[...] = jnp.abs(times - times.T)
    buckets = rab_s.shape[1]
    for b in range(4):
        where = slice(b * count // 4, (b + 1) * count // 4)
        gaps = gap[where]

        def look(d, sums):
            for e in range(4):
                here = gaps == d * 4 + e
                sums = tuple(jnp.where(here, rab_s[n, d * 4 + e], s) for n, s in enumerate(sums))
            return sums

        found = lax.fori_loop(0, buckets // 4, look, (jnp.zeros(gaps.shape, F32),) * heads)
        for n in range(heads):
            bias[n, where] = found[n]
        step_x(order[3 + b])
    seg_row, seg_col = jnp.zeros((count, count), jnp.int32), jnp.zeros((count, count), jnp.int32)
    place_col = iota((count, 1), 0)
    valid = jnp.ones((count, 1), F32)
    end = 0
    for s in range(len_s.shape[1]):
        end = end + len_s[0, s]
        seg_row += jnp.where(col >= end, 1, 0)
        seg_col += jnp.where(row >= end, 1, 0)
        valid = jnp.where(place_col + 1 == end, 0.0, valid)
    allowed = jnp.where((col <= row) & (seg_row == seg_col), 1.0 / MOST_LEN, 0.0)
    valid = jnp.where(place_col + 1 == count, 0.0, valid)

    for dy in order[7:]:
        step_x(dy)

    def given():
        return remote(
            served.at[pl.ds(0, (groups - 1) * 8)], recv.at[pl.ds(0, (groups - 1) * 8)], row_sems.at[0], row_sems.at[1],
            {"group": me},
        )

    given().wait_recv()
    slot_lane = iota((count, slots), 1)
    for q in range(2):
        emb[:, q * half : (q + 1) * half] = select_dot(hot(slot_lane == slot_col + 4 * q), recv[...])
    e = emb[...]
    e = e - rows_sum(e) / width
    scale1 = lax.rsqrt(rows_sum(e * e) / width + 1e-05)
    norm[...] = e * scale1
    for c in range(4):
        part_c = slice(c * width, (c + 1) * width)
        pre = mul3(norm[...], in_hi[:, part_c], in_lo[:, part_c]) + b_in_v[:, part_c]
        sig = 1.0 / (1.0 + jnp.exp(-pre))
        hid[:, part_c] = pre * sig
        slope[:, part_c] = sig * (1.0 + pre * (1.0 - sig))
    for dy in order:
        block = at(x + 2, y + dy, core)
        arrive(block)
        pass_on(block, sibling)
    size = width // heads
    root = size ** (-0.5)

    def head(part_c, n):
        return slice(part_c * width + n * size, part_c * width + (n + 1) * size)

    for n in range(heads):
        score = mul3(hid[:, head(2, n)], *weights_of(hid[:, head(3, n)]), NT) * root + bias[n]
        sig = 1.0 / (1.0 + jnp.exp(-score))
        weight = score * sig * allowed
        attn[n] = weight
        attn_slope[n] = sig * (1.0 + score * (1.0 - sig)) * allowed
        mixed[:, head(0, n)] = mul3(weight, *weights_of(hid[:, head(1, n)]))
    m = mixed[...]
    m = m - rows_sum(m) / width
    scale2 = lax.rsqrt(rows_sum(m * m) / width + 1e-05)
    mixed[...] = m * scale2
    out = mul3(mixed[...] * hid[:, :width], out_hi[...], out_lo[...]) + emb[...]
    scale3 = lax.rsqrt(rows_sum(out * out) + 1e-06)
    state = out * scale3
    e = emb[...]
    row_col = iota((count, width), 0)
    after = jnp.where(row_col == count - 1, 0.0, pltpu.roll(e, count - 1, 0))
    scale4 = lax.rsqrt(rows_sum(after * after) + 1e-06)
    target = after * scale4
    positive = rows_sum(state * target) / TEMPER
    zneg = jnp.zeros((count, 1), F32)
    pulled = jnp.zeros((count, width), F32)
    state_hi, state_lo = weights_of(state)
    state_two = jnp.concatenate([state_hi, state_lo], axis=0)
    for dx in (0, -1, 1, 2):
        for dy in range(ny):
            arrive(at(x + dx, y + dy, 1 - core))
        block = panel[rows8(lax.rem(x + dx + nx, nx), 2 * ny * nneg)]
        high, low = weights_of(block)
        logit = lax.dot_general(state_two, high, NT, preferred_element_type=F32)
        logit = logit[:count] + logit[count:] + lax.dot_general(state_hi, low, NT, preferred_element_type=F32)
        exps = jnp.exp(logit / TEMPER)
        zneg += rows_sum(exps)
        pulled += mul3(exps, high, low)
    expos = jnp.exp(positive)
    total = expos + zneg
    loss = valid * (jnp.log(total) - positive)
    loss_ref[...] = jnp.broadcast_to(loss, (count, count)).T[:1]
    share = expos / total - 1.0
    weigh = valid / TEMPER
    d_state = weigh * (share * target + pulled / total)
    d_target = (weigh * share) * state
    d_out = scale3 * (d_state - state * rows_sum(state * d_state))
    d_after = scale4 * (d_target - target * rows_sum(target * d_target))
    d_emb = d_out + jnp.where(row_col == 0, 0.0, pltpu.roll(d_after, 1, 0))
    emb[...] = d_emb
    d_gated = mul3(d_out, out_hi[...], out_lo[...], NT)
    dhid[:, :width] = d_gated * mixed[...] * slope[:, :width]
    mixed[...] = norm_back(d_gated * hid[:, :width], mixed[...], scale2)
    for n in range(heads):
        d_mix = mixed[:, head(0, n)]
        weight = attn[n]
        d_weight = mul3(d_mix, *weights_of(hid[:, head(1, n)]), NT)
        d_score = d_weight * attn_slope[n] * root
        mix_hi, mix_lo = weights_of(d_mix)
        dhid[:, head(1, n)] = mul3(weight.T, mix_hi, mix_lo) * slope[:, head(1, n)]
        dhid[:, head(2, n)] = mul3(d_score, *weights_of(hid[:, head(3, n)])) * slope[:, head(2, n)]
        dhid[:, head(3, n)] = mul3(d_score.T, *weights_of(hid[:, head(2, n)])) * slope[:, head(3, n)]
    d_norm = mul3(dhid[:, :width], in_hi[:, :width], in_lo[:, :width], NT)
    for c in range(1, 4):
        part_c = slice(c * width, (c + 1) * width)
        d_norm += mul3(dhid[:, part_c], in_hi[:, part_c], in_lo[:, part_c], NT)
    emb[...] += norm_back(d_norm, norm[...], scale1)
    chunks = outgoing.shape[0]
    z_order = sorted(range(1, shards), key=lambda k: -min(k, shards - k))
    for h in range(chunks):
        cols = [slice((2 * h + q) * 128, (2 * h + q + 1) * 128) for q in range(2)]
        outgoing[h] = select_dot(place[...], jnp.concatenate([emb[:, c] for c in cols], axis=0))

        def send(k, c):
            peer = nth_peer(k)
            remote(
                outgoing.at[h, rows8(peer)], incoming.at[h, rows8(me)], send_sem.at[h], recv_sem.at[h], {"group": peer}
            ).start()
            return c

        lax.fori_loop(0, groups - 1, send, 0)
        incoming[h, rows8(me)] = outgoing[h, rows8(me)]

    def whole(h):
        where = pl.ds(0, (groups - 1) * 8)
        return remote(outgoing.at[h, where], incoming.at[h, where], send_sem.at[h], recv_sem.at[h], {"group": me})

    for h in range(chunks):
        whole(h).wait_recv()
        spare = part.shape[1] - 2 * 128
        part[h, pl.ds(2 * 128, spare)] = jnp.zeros((spare, 128), F32)
        for q in range(2):
            part[h, pl.ds(q * 128, 128)] = select_dot(picks[q], incoming[h])

        for k in z_order:
            peer = lax.rem(my + k, shards)
            remote(part.at[h, rows8(peer, piece)], rsum.at[h, my], rs_send.at[h], rs_recv.at[h], {"shard": peer}).start()
        rsum[h, my] = part[h, rows8(my, piece)]

    def whole_rs(h):
        where = pl.ds(0, shards - 1)
        return remote(rsum.at[h, where], rsum.at[h, where], rs_send.at[h], rs_recv.at[h], {"shard": my})

    own = rows8(my, piece)
    for h in range(chunks):
        whole_rs(h).wait_recv()
        red_ref[h, own] = jnp.sum(rsum[h], axis=0)

        for k in z_order:
            peer = lax.rem(my + k, shards)
            remote(red_ref.at[h, own], red_ref.at[h, own], ag_send.at[h], ag_recv.at[h], {"shard": peer}).start()
    for h in range(chunks):
        where = pl.ds(0, (shards - 1) * piece)
        tail = remote(red_ref.at[h, where], red_ref.at[h, where], ag_send.at[h], ag_recv.at[h], {"shard": my})
        tail.wait_recv()
        tail.wait_send()
        whole(h).wait_send()
        whole_rs(h).wait_send()
    told().wait_send()
    given().wait_send()
    sent = pl.ds(0, (groups - 1) * nneg)
    remote(panel.at[sent], panel.at[sent], neg_send, neg_recv.at[0], {"group": me}).wait_send()


def body(item_ids, seq_lengths, time_buckets, neg_ids, table, w_in, b_in, w_out, rab):
    groups, shards = lax.axis_size("group"), lax.axis_size("shard")
    count, width = item_ids.shape[0], table.shape[1]
    heads, hidden = rab.shape[0], w_in.shape[1]
    nneg = neg_ids.shape[1]
    slots, chunks = groups * 8, width // 256
    piece = (-(-256 // shards) + 7) // 8 * 8
    red_rows = shards * piece
    vm, smem, dma, i32 = pltpu.VMEM, pltpu.SMEM, pltpu.SemaphoreType.DMA, jnp.int32
    anywhere = pl.BlockSpec(memory_space=pl.ANY)
    red, loss = pl.pallas_call(
        functools.partial(step_kernel, (groups // 16, 8), shards, piece, heads),
        out_shape=(
            jax.ShapeDtypeStruct((chunks, red_rows, 128), F32),
            jax.ShapeDtypeStruct((1, count), F32),
        ),
        in_specs=[anywhere] * 9,
        out_specs=(pl.BlockSpec(memory_space=vm),) * 2,
        scratch_shapes=[
            vm((1, count), i32),
            smem(seq_lengths.shape, i32),
            vm((1, count), i32),
            vm((1, nneg), i32),
            vm(table.shape, F32),
            vm(w_in.shape, F32),
            vm((1, hidden), F32),
            vm(w_out.shape, F32),
            smem(rab.shape, F32),
            dma((9,)),
            vm(w_in.shape, BF16),
            vm(w_in.shape, BF16),
            vm(w_out.shape, BF16),
            vm(w_out.shape, BF16),
            vm((groups * nneg, width), F32),
            vm((groups, 1, count), i32),
            vm((slots, count), i32),
            vm((slots, width // 2), F32),
            vm((slots, width // 2), F32),
            vm((slots, 2 * count), BF16),
            vm((2, count, slots), BF16),
            vm((count, width), F32),
            vm((count, width), F32),
            vm((count, hidden), F32),
            vm((count, hidden), F32),
            vm((count, count), i32),
            vm((heads, count, count), F32),
            vm((heads, count, count), F32),
            vm((heads, count, count), F32),
            vm((count, width), F32),
            vm((count, hidden), F32),
            vm((chunks, slots, 128), F32),
            vm((chunks, slots, 128), F32),
            vm((chunks, red_rows, 128), F32),
            vm((chunks, shards, piece, 128), F32),
            dma((2,)),
            dma((2,)),
            dma,
            dma((groups,)),
        ]
        + [dma((chunks,))] * 6,
        compiler_params=pltpu.CompilerParams(collective_id=0, has_side_effects=True, vmem_limit_bytes=56 << 20),
        name="hstu_step",
    )(
        item_ids.reshape(1, -1), seq_lengths, time_buckets.reshape(1, -1), neg_ids, table, w_in, b_in.reshape(1, -1), w_out,
        rab,
    )
    parts = red[:, :256].reshape(chunks * 2, count, 128)
    return parts.transpose(1, 0, 2).reshape(count, width), loss.reshape(-1)


def solution(mesh):
    in_specs = (
        P(("shard", "group")),
        P(("shard", "group"), None),
        P(("shard", "group")),
        P("shard", "group"),
        P("group", None),
        P(),
        P(),
        P(),
        P(),
    )
    out_specs = (P("group", None), P(("shard", "group")))
    return jax.shard_map(body, mesh=mesh, in_specs=in_specs, out_specs=out_specs, check_vma=False)
```

```python
import functools

import jax
import jax.numpy as jnp
from jax import lax
from jax.experimental import pallas as pl
from jax.experimental.pallas import tpu as pltpu
from jax.sharding import PartitionSpec as P

MOST_LEN = 64
TEMPER = 0.05
MESH = pl.DeviceIdType.MESH
F32 = jnp.float32
BF16 = jnp.bfloat16


def pieces_of(value, count):
    terms = []
    for _ in range(count):
        term = value.astype(BF16)
        terms.append(term)
        value = value - term.astype(F32)
    return terms


def select_dot(onehot, value, count=3):
    return sum(jnp.dot(onehot, term, preferred_element_type=F32) for term in pieces_of(value, count))


def iota(shape, dim):
    return lax.broadcasted_iota(jnp.int32, shape, dim)


def hot(mask):
    return mask.astype(F32).astype(BF16)


def greet(sem, device):
    pl.semaphore_signal(sem, inc=1, device_id=device, device_id_type=MESH)


def remote(src, dst, send_sem, recv_sem, device):
    return pltpu.make_async_remote_copy(
        src_ref=src, dst_ref=dst, send_sem=send_sem, recv_sem=recv_sem, device_id=device, device_id_type=MESH
    )


def rows8(index, rows=8):
    return pl.ds(pl.multiple_of(index * rows, rows), rows)


def weights_of(value):
    high = value.astype(BF16)
    return high, (value - high.astype(F32)).astype(BF16)


NN = (((1,), (0,)), ((), ()))
NT = (((1,), (1,)), ((), ()))


def mul3(left, high, low, dims=NN):
    count = left.shape[0]
    lhigh, llow = weights_of(left)
    both = lax.dot_general(jnp.concatenate([lhigh, llow], axis=0), high, dims, preferred_element_type=F32)
    return both[:count] + both[count:] + lax.dot_general(lhigh, low, dims, preferred_element_type=F32)


def rows_sum(value):
    return jnp.sum(value, axis=-1, keepdims=True)


def norm_back(d_norm, norm, scale):
    width = norm.shape[-1]
    return scale * (d_norm - rows_sum(d_norm) / width - norm * (rows_sum(d_norm * norm) / width))


def step_kernel(
    dims, shards, piece, heads,
    ids_h, len_h, time_h, neg_h, table_h, w_in_h, b_in_h, w_out_h, rab_h,
    red_ref, loss_ref,
    ids_v, len_s, time_v, neg_v, table_v, w_in_v, b_in_v, w_out_v, rab_s, load_sems,
    in_hi, in_lo, out_hi, out_lo, panel,
    ids_all, expand, served, recv, place, picks,
    emb, norm, hid, slope, gap, bias, attn, attn_slope, mixed, dhid,
    outgoing, incoming, part, rsum,
    id_sems, row_sems, neg_send, neg_recv, send_sem, recv_sem, rs_send, rs_recv, ag_send, ag_recv,
):
    nx, ny = dims
    groups = nx * ny * 2
    count = ids_v.shape[1]
    width = table_v.shape[1]
    nneg = neg_v.shape[1]
    slots = groups * 8
    me, my = lax.axis_index("group"), lax.axis_index("shard")
    core = lax.rem(me, 2)
    x, y = me // (2 * ny), lax.rem(me // 2, ny)

    def at(xx, yy, cc):
        return (lax.rem(xx + nx, nx) * ny + lax.rem(yy + ny, ny)) * 2 + cc

    barrier = pltpu.get_barrier_semaphore()
    pairs = [
        (ids_h, ids_v), (table_h, table_v), (neg_h, neg_v), (len_h, len_s), (time_h, time_v), (rab_h, rab_s),
        (w_in_h, w_in_v), (w_out_h, w_out_v), (b_in_h, b_in_v),
    ]
    loads = [pltpu.make_async_copy(a, b, load_sems.at[i]) for i, (a, b) in enumerate(pairs)]
    for load in loads:
        load.start()

    def hello(k, c):
        greet(barrier, {"group": lax.rem(me + k, groups)})
        return c

    lax.fori_loop(1, groups, hello, 0)

    def hello_z(k, c):
        greet(barrier, {"shard": lax.rem(my + k, shards)})
        return c

    lax.fori_loop(1, shards, hello_z, 0)
    loads[0].wait()
    rows_dev = table_v.shape[0]
    ids_all[me] = ids_v[...]
    pl.semaphore_wait(barrier, groups - 1 + shards - 1)

    def fold(i, n):
        return jnp.where(lax.rem(i, 2) == 1, n // 2 - (i + 1) // 2, n // 2 + i // 2)

    def nth_peer(k):
        return at(x + fold(lax.rem(k, 2 * nx) // 2, nx), y + fold(k // (2 * nx), ny), lax.rem(core + 1 - lax.rem(k, 2), 2))

    def tell(k, c):
        remote(ids_all.at[me], ids_all.at[me], id_sems.at[0], id_sems.at[1], {"group": nth_peer(k)}).start()
        return c

    lax.fori_loop(0, groups - 1, tell, 0)
    loads[1].wait()
    loads[2].wait()
    neg_row = lax.rem(neg_v[...], rows_dev)
    neg_hot = hot(jnp.broadcast_to(neg_row, (rows_dev, nneg)) == iota((rows_dev, nneg), 0)).T
    drawn = select_dot(neg_hot, table_v[...])
    mine = rows8(me, nneg)
    panel[mine] = drawn * lax.rsqrt(rows_sum(drawn * drawn) + 1e-06)

    def pass_on(block, device):
        where = rows8(block, nneg)
        remote(panel.at[where], panel.at[where], neg_send, neg_recv.at[block], {"group": device}).start()

    def arrive(block):
        where = rows8(block, nneg)
        remote(panel.at[where], panel.at[where], neg_send, neg_recv.at[block], {"group": me}).wait_recv()

    sibling = at(x, y, 1 - core)

    def across_x(block):
        pass_on(block, at(x + 1, y, core))
        pass_on(block, at(x - 1, y, core))

    for dy in (1, -1, 2, -2):
        pass_on(me, at(x, y + dy, core))

    def told():
        where = pl.ds(0, groups - 1)
        return remote(ids_all.at[where], ids_all.at[where], id_sems.at[0], id_sems.at[1], {"group": me})

    across_x(me)
    pass_on(me, sibling)
    def step_y(dy, onward=()):
        block = at(x, y + dy, core)
        arrive(block)
        for to in onward:
            pass_on(block, at(x, y + to, core))
        across_x(block)
        pass_on(block, sibling)

    step_y(-1)
    step_y(1)
    step_y(-2, (2, 1))
    step_y(2, (-1,))
    told().wait_recv()

    def widen(g, c):
        expand[rows8(g)] = jnp.broadcast_to(ids_all[g], (8, count))
        return c

    lax.fori_loop(0, groups, widen, 0)
    col, row = iota((count, count), 1), iota((count, count), 0)
    lanes, subs = iota((slots, count), 1), lax.rem(iota((slots, count), 0), 8)
    asked = expand[...]
    here = asked // rows_dev == me
    earlier = hot(row < col)
    turn = jnp.dot(hot(here), earlier, preferred_element_type=F32).astype(jnp.int32)
    kept = jnp.where(here & (turn == lax.rem(subs, 4)), asked - me * rows_dev + 1, 0).astype(F32).astype(BF16)
    ones = jnp.ones((count, count), BF16)
    named = jnp.dot(kept, ones, preferred_element_type=F32).astype(jnp.int32)
    fits = named == lanes + 1
    serve = jnp.concatenate([hot(fits & (subs < 4)), hot(fits & (subs >= 4))], axis=1)
    half = width // 2
    stacked = jnp.concatenate([table_v[:, :half], table_v[:, half:]], axis=0)
    served[...] = select_dot(serve, stacked)

    def give(k, c):
        peer = nth_peer(k)
        remote(served.at[rows8(peer)], recv.at[rows8(me)], row_sems.at[0], row_sems.at[1], {"group": peer}).start()
        return c

    recv[rows8(me)] = served[rows8(me)]
    lax.fori_loop(0, groups - 1, give, 0)
    for dy in (-3, 3, -4):
        step_y(dy)
    order = [0, -1, 1, -2, 2, -3, 3, -4]

    def step_x(dy):
        for dx in (-1, 1):
            block = at(x + dx, y + dy, core)
            arrive(block)
            if (dy % 2 == 0) == (dx < 0):
                pass_on(block, at(x - dx, y, core))
            pass_on(block, sibling)

    step_x(order[0])
    ids = jnp.broadcast_to(ids_v[...], (count, count))
    ids_t = ids.T
    own_row, own_col = ids // rows_dev, ids_t // rows_dev
    same = own_row == own_col
    rank_col = jnp.sum(jnp.where(same & (col < row), 1, 0), axis=1, keepdims=True)
    rank_row = jnp.sum(jnp.where(same & (row < col), 1, 0), axis=0, keepdims=True)
    slot_col = own_col[:, :1] * 8 + rank_col
    slot_row = own_row[:1] * 8 + rank_row
    named_t = lax.dot_general(ones, kept, NT, preferred_element_type=F32).astype(jnp.int32)
    fits_t = named_t == iota((count, slots), 0) + 1
    subs_t = lax.rem(iota((count, slots), 1), 8)
    picks[0] = hot(fits_t & (subs_t < 4))
    picks[1] = hot(fits_t & (subs_t >= 4))
    slot_sub = iota((slots, count), 0)
    place[:, :count] = hot(slot_sub == slot_row)
    place[:, count:] = hot(slot_sub == slot_row + 4)
    for load in loads[3:]:
        load.wait()
    step_x(order[1])

    def refine(source, high, low):
        def body(i, c):
            where = rows8(i, 32)
            high[where], low[where] = weights_of(source[where])
            return c

        lax.fori_loop(0, width // 32, body, 0)

    refine(w_in_v, in_hi, in_lo)
    step_x(order[2])
    refine(w_out_v, out_hi, out_lo)
    times = jnp.broadcast_to(time_v[...], (count, count))
    gap[...] = jnp.abs(times - times.T)
    buckets = rab_s.shape[1]
    for b in range(4):
        where = slice(b * count // 4, (b + 1) * count // 4)
        gaps = gap[where]

        def look(d, sums):
            for e in range(4):
                here = gaps == d * 4 + e
                sums = tuple(jnp.where(here, rab_s[n, d * 4 + e], s) for n, s in enumerate(sums))
            return sums

        found = lax.fori_loop(0, buckets // 4, look, (jnp.zeros(gaps.shape, F32),) * heads)
        for n in range(heads):
            bias[n, where] = found[n]
        step_x(order[3 + b])
    seg_row, seg_col = jnp.zeros((count, count), jnp.int32), jnp.zeros((count, count), jnp.int32)
    place_col = iota((count, 1), 0)
    valid = jnp.ones((count, 1), F32)
    end = 0
    for s in range(len_s.shape[1]):
        end = end + len_s[0, s]
        seg_row += jnp.where(col >= end, 1, 0)
        seg_col += jnp.where(row >= end, 1, 0)
        valid = jnp.where(place_col + 1 == end, 0.0, valid)
    allowed = jnp.where((col <= row) & (seg_row == seg_col), 1.0 / MOST_LEN, 0.0)
    valid = jnp.where(place_col + 1 == count, 0.0, valid)

    for dy in order[7:]:
        step_x(dy)

    def given():
        return remote(
            served.at[pl.ds(0, (groups - 1) * 8)], recv.at[pl.ds(0, (groups - 1) * 8)], row_sems.at[0], row_sems.at[1],
            {"group": me},
        )

    given().wait_recv()
    slot_lane = iota((count, slots), 1)
    for q in range(2):
        emb[:, q * half : (q + 1) * half] = select_dot(hot(slot_lane == slot_col + 4 * q), recv[...])
    e = emb[...]
    e = e - rows_sum(e) / width
    scale1 = lax.rsqrt(rows_sum(e * e) / width + 1e-05)
    norm[...] = e * scale1
    for c in range(4):
        part_c = slice(c * width, (c + 1) * width)
        pre = mul3(norm[...], in_hi[:, part_c], in_lo[:, part_c]) + b_in_v[:, part_c]
        sig = 1.0 / (1.0 + jnp.exp(-pre))
        hid[:, part_c] = pre * sig
        slope[:, part_c] = sig * (1.0 + pre * (1.0 - sig))
    for dy in order:
        block = at(x + 2, y + dy, core)
        arrive(block)
        pass_on(block, sibling)
    size = width // heads
    root = size ** (-0.5)

    def head(part_c, n):
        return slice(part_c * width + n * size, part_c * width + (n + 1) * size)

    for n in range(heads):
        score = mul3(hid[:, head(2, n)], *weights_of(hid[:, head(3, n)]), NT) * root + bias[n]
        sig = 1.0 / (1.0 + jnp.exp(-score))
        weight = score * sig * allowed
        attn[n] = weight
        attn_slope[n] = sig * (1.0 + score * (1.0 - sig)) * allowed
        mixed[:, head(0, n)] = mul3(weight, *weights_of(hid[:, head(1, n)]))
    m = mixed[...]
    m = m - rows_sum(m) / width
    scale2 = lax.rsqrt(rows_sum(m * m) / width + 1e-05)
    mixed[...] = m * scale2
    out = mul3(mixed[...] * hid[:, :width], out_hi[...], out_lo[...]) + emb[...]
    scale3 = lax.rsqrt(rows_sum(out * out) + 1e-06)
    state = out * scale3
    e = emb[...]
    row_col = iota((count, width), 0)
    after = jnp.where(row_col == count - 1, 0.0, pltpu.roll(e, count - 1, 0))
    scale4 = lax.rsqrt(rows_sum(after * after) + 1e-06)
    target = after * scale4
    positive = rows_sum(state * target) / TEMPER
    zneg = jnp.zeros((count, 1), F32)
    pulled = jnp.zeros((count, width), F32)
    state_hi, state_lo = weights_of(state)
    state_two = jnp.concatenate([state_hi, state_lo], axis=0)
    for dx in (0, -1, 1, 2):
        for dy in range(ny):
            arrive(at(x + dx, y + dy, 1 - core))
        block = panel[rows8(lax.rem(x + dx + nx, nx), 2 * ny * nneg)]
        high, low = weights_of(block)
        logit = lax.dot_general(state_two, high, NT, preferred_element_type=F32)
        logit = logit[:count] + logit[count:] + lax.dot_general(state_hi, low, NT, preferred_element_type=F32)
        exps = jnp.exp(logit / TEMPER)
        zneg += rows_sum(exps)
        pulled += mul3(exps, high, low)
    expos = jnp.exp(positive)
    total = expos + zneg
    loss = valid * (jnp.log(total) - positive)
    loss_ref[...] = jnp.broadcast_to(loss, (count, count)).T[:1]
    share = expos / total - 1.0
    weigh = valid / TEMPER
    d_state = weigh * (share * target + pulled / total)
    d_target = (weigh * share) * state
    d_out = scale3 * (d_state - state * rows_sum(state * d_state))
    d_after = scale4 * (d_target - target * rows_sum(target * d_target))
    d_emb = d_out + jnp.where(row_col == 0, 0.0, pltpu.roll(d_after, 1, 0))
    emb[...] = d_emb
    d_gated = mul3(d_out, out_hi[...], out_lo[...], NT)
    dhid[:, :width] = d_gated * mixed[...] * slope[:, :width]
    mixed[...] = norm_back(d_gated * hid[:, :width], mixed[...], scale2)
    for n in range(heads):
        d_mix = mixed[:, head(0, n)]
        weight = attn[n]
        d_weight = mul3(d_mix, *weights_of(hid[:, head(1, n)]), NT)
        d_score = d_weight * attn_slope[n] * root
        mix_hi, mix_lo = weights_of(d_mix)
        dhid[:, head(1, n)] = mul3(weight.T, mix_hi, mix_lo) * slope[:, head(1, n)]
        dhid[:, head(2, n)] = mul3(d_score, *weights_of(hid[:, head(3, n)])) * slope[:, head(2, n)]
        dhid[:, head(3, n)] = mul3(d_score.T, *weights_of(hid[:, head(2, n)])) * slope[:, head(3, n)]
    d_norm = mul3(dhid[:, :width], in_hi[:, :width], in_lo[:, :width], NT)
    for c in range(1, 4):
        part_c = slice(c * width, (c + 1) * width)
        d_norm += mul3(dhid[:, part_c], in_hi[:, part_c], in_lo[:, part_c], NT)
    emb[...] += norm_back(d_norm, norm[...], scale1)
    chunks = outgoing.shape[0]
    last = shards - 1
    z_order = sorted(range(1, shards), key=lambda k: -min(k, shards - k))
    for h in range(chunks):
        cols = [slice((2 * h + q) * 128, (2 * h + q + 1) * 128) for q in range(2)]
        outgoing[h] = select_dot(place[...], jnp.concatenate([emb[:, c] for c in cols], axis=0))

        def send(k, c):
            peer = nth_peer(k)
            remote(
                outgoing.at[h, rows8(peer)], incoming.at[h, rows8(me)], send_sem.at[h], recv_sem.at[h], {"group": peer}
            ).start()
            return c

        lax.fori_loop(0, groups - 1, send, 0)
        incoming[h, rows8(me)] = outgoing[h, rows8(me)]

    def whole(h):
        where = pl.ds(0, (groups - 1) * 8)
        return remote(outgoing.at[h, where], incoming.at[h, where], send_sem.at[h], recv_sem.at[h], {"group": me})

    for h in range(chunks):
        whole(h).wait_recv()
        spare = part.shape[1] - 2 * 128
        part[h, pl.ds(2 * 128, spare)] = jnp.zeros((spare, 128), F32)
        for q in range(2):
            part[h, pl.ds(q * 128, 128)] = select_dot(picks[q], incoming[h])

        for k in z_order:
            peer = lax.rem(my + k, shards)

            @pl.when(peer != last)
            def _():
                remote(
                    part.at[h, rows8(peer, piece)], rsum.at[h, my], rs_send.at[h], rs_recv.at[h], {"shard": peer}
                ).start()

        rsum[h, my] = part[h, rows8(my, piece)]

    def some_rs(h, pieces):
        where = pl.ds(0, pieces)
        return remote(rsum.at[h, where], rsum.at[h, where], rs_send.at[h], rs_recv.at[h], {"shard": my})

    def some_red(h, pieces):
        where = pl.ds(0, pieces * piece)
        return remote(red_ref.at[h, where], red_ref.at[h, where], ag_send.at[h], ag_recv.at[h], {"shard": my})

    own = rows8(my, piece)
    for h in range(chunks):

        @pl.when(my != last)
        def _():
            some_rs(h, shards - 1).wait_recv()
            red_ref[h, own] = jnp.sum(rsum[h], axis=0)
            for k in z_order:
                peer = lax.rem(my + k, shards)
                remote(red_ref.at[h, own], red_ref.at[h, own], ag_send.at[h], ag_recv.at[h], {"shard": peer}).start()

    for h in range(chunks):

        @pl.when(my != last)
        def _():
            some_red(h, shards - 2).wait_recv()
            some_red(h, shards - 1).wait_send()
            some_rs(h, shards - 2).wait_send()

        @pl.when(my == last)
        def _():
            some_red(h, shards - 1).wait_recv()
            some_rs(h, shards - 1).wait_send()

        whole(h).wait_send()
    told().wait_send()
    given().wait_send()
    sent = pl.ds(0, (groups - 1) * nneg)
    remote(panel.at[sent], panel.at[sent], neg_send, neg_recv.at[0], {"group": me}).wait_send()


def body(item_ids, seq_lengths, time_buckets, neg_ids, table, w_in, b_in, w_out, rab):
    groups, shards = lax.axis_size("group"), lax.axis_size("shard")
    count, width = item_ids.shape[0], table.shape[1]
    heads, hidden = rab.shape[0], w_in.shape[1]
    nneg = neg_ids.shape[1]
    slots, chunks = groups * 8, width // 256
    piece = (-(-256 // shards) + 7) // 8 * 8
    red_rows = shards * piece
    vm, smem, dma, i32 = pltpu.VMEM, pltpu.SMEM, pltpu.SemaphoreType.DMA, jnp.int32
    anywhere = pl.BlockSpec(memory_space=pl.ANY)
    red, loss = pl.pallas_call(
        functools.partial(step_kernel, (groups // 16, 8), shards, piece, heads),
        out_shape=(
            jax.ShapeDtypeStruct((chunks, red_rows, 128), F32),
            jax.ShapeDtypeStruct((1, count), F32),
        ),
        in_specs=[anywhere] * 9,
        out_specs=(pl.BlockSpec(memory_space=vm),) * 2,
        scratch_shapes=[
            vm((1, count), i32),
            smem(seq_lengths.shape, i32),
            vm((1, count), i32),
            vm((1, nneg), i32),
            vm(table.shape, F32),
            vm(w_in.shape, F32),
            vm((1, hidden), F32),
            vm(w_out.shape, F32),
            smem(rab.shape, F32),
            dma((9,)),
            vm(w_in.shape, BF16),
            vm(w_in.shape, BF16),
            vm(w_out.shape, BF16),
            vm(w_out.shape, BF16),
            vm((groups * nneg, width), F32),
            vm((groups, 1, count), i32),
            vm((slots, count), i32),
            vm((slots, width // 2), F32),
            vm((slots, width // 2), F32),
            vm((slots, 2 * count), BF16),
            vm((2, count, slots), BF16),
            vm((count, width), F32),
            vm((count, width), F32),
            vm((count, hidden), F32),
            vm((count, hidden), F32),
            vm((count, count), i32),
            vm((heads, count, count), F32),
            vm((heads, count, count), F32),
            vm((heads, count, count), F32),
            vm((count, width), F32),
            vm((count, hidden), F32),
            vm((chunks, slots, 128), F32),
            vm((chunks, slots, 128), F32),
            vm((chunks, red_rows, 128), F32),
            vm((chunks, shards, piece, 128), F32),
            dma((2,)),
            dma((2,)),
            dma,
            dma((groups,)),
        ]
        + [dma((chunks,))] * 6,
        compiler_params=pltpu.CompilerParams(collective_id=0, has_side_effects=True, vmem_limit_bytes=56 << 20),
        name="hstu_step",
    )(
        item_ids.reshape(1, -1), seq_lengths, time_buckets.reshape(1, -1), neg_ids, table, w_in, b_in.reshape(1, -1), w_out,
        rab,
    )
    parts = red[:, :256].reshape(chunks * 2, count, 128)
    return parts.transpose(1, 0, 2).reshape(count, width), loss.reshape(-1)


def solution(mesh):
    in_specs = (
        P(("shard", "group")),
        P(("shard", "group"), None),
        P(("shard", "group")),
        P("shard", "group"),
        P("group", None),
        P(),
        P(),
        P(),
        P(),
    )
    out_specs = (P("group", None), P(("shard", "group")))
    return jax.shard_map(body, mesh=mesh, in_specs=in_specs, out_specs=out_specs, check_vma=False)
```

```python
import functools

import jax
import jax.numpy as jnp
from jax import lax
from jax.experimental import pallas as pl
from jax.experimental.pallas import tpu as pltpu
from jax.sharding import PartitionSpec as P

MOST_LEN = 64
TEMPER = 0.05
MESH = pl.DeviceIdType.MESH
F32 = jnp.float32
BF16 = jnp.bfloat16


def pieces_of(value, count):
    terms = []
    for _ in range(count):
        term = value.astype(BF16)
        terms.append(term)
        value = value - term.astype(F32)
    return terms


def select_dot(onehot, value, count=3):
    return sum(jnp.dot(onehot, term, preferred_element_type=F32) for term in pieces_of(value, count))


def iota(shape, dim):
    return lax.broadcasted_iota(jnp.int32, shape, dim)


def hot(mask):
    return mask.astype(F32).astype(BF16)


def greet(sem, device):
    pl.semaphore_signal(sem, inc=1, device_id=device, device_id_type=MESH)


def remote(src, dst, send_sem, recv_sem, device):
    return pltpu.make_async_remote_copy(
        src_ref=src, dst_ref=dst, send_sem=send_sem, recv_sem=recv_sem, device_id=device, device_id_type=MESH
    )


def rows8(index, rows=8):
    return pl.ds(pl.multiple_of(index * rows, rows), rows)


def weights_of(value):
    high = value.astype(BF16)
    return high, (value - high.astype(F32)).astype(BF16)


NN = (((1,), (0,)), ((), ()))
NT = (((1,), (1,)), ((), ()))


def mul3(left, high, low, dims=NN):
    count = left.shape[0]
    lhigh, llow = weights_of(left)
    both = lax.dot_general(jnp.concatenate([lhigh, llow], axis=0), high, dims, preferred_element_type=F32)
    return both[:count] + both[count:] + lax.dot_general(lhigh, low, dims, preferred_element_type=F32)


def rows_sum(value):
    return jnp.sum(value, axis=-1, keepdims=True)


def norm_back(d_norm, norm, scale):
    width = norm.shape[-1]
    return scale * (d_norm - rows_sum(d_norm) / width - norm * (rows_sum(d_norm * norm) / width))


def step_kernel(
    dims, shards, piece, heads,
    ids_h, len_h, time_h, neg_h, table_h, w_in_h, b_in_h, w_out_h, rab_h,
    red_ref, loss_ref,
    ids_v, len_s, time_v, neg_v, table_v, w_in_v, b_in_v, w_out_v, rab_s, load_sems,
    in_hi, in_lo, out_hi, out_lo, panel,
    ids_all, expand, served, recv, place, picks,
    emb, norm, hid, slope, gap, bias, attn, attn_slope, mixed, dhid,
    outgoing, incoming, part, rsum,
    id_sems, row_sems, neg_send, neg_recv, send_sem, recv_sem, rs_send, rs_recv, ag_send, ag_recv,
):
    nx, ny = dims
    groups = nx * ny * 2
    count = ids_v.shape[1]
    width = table_v.shape[1]
    nneg = neg_v.shape[1]
    slots = groups * 8
    me, my = lax.axis_index("group"), lax.axis_index("shard")
    core = lax.rem(me, 2)
    x, y = me // (2 * ny), lax.rem(me // 2, ny)

    def at(xx, yy, cc):
        return (lax.rem(xx + nx, nx) * ny + lax.rem(yy + ny, ny)) * 2 + cc

    barrier = pltpu.get_barrier_semaphore()
    pairs = [
        (ids_h, ids_v), (table_h, table_v), (neg_h, neg_v), (len_h, len_s), (time_h, time_v), (rab_h, rab_s),
        (w_in_h, w_in_v), (w_out_h, w_out_v), (b_in_h, b_in_v),
    ]
    loads = [pltpu.make_async_copy(a, b, load_sems.at[i]) for i, (a, b) in enumerate(pairs)]
    for load in loads:
        load.start()

    def hello(k, c):
        greet(barrier, {"group": lax.rem(me + k, groups)})
        return c

    lax.fori_loop(1, groups, hello, 0)

    def hello_z(k, c):
        greet(barrier, {"shard": lax.rem(my + k, shards)})
        return c

    lax.fori_loop(1, shards, hello_z, 0)
    loads[0].wait()
    rows_dev = table_v.shape[0]
    ids_all[me] = ids_v[...]
    pl.semaphore_wait(barrier, groups - 1 + shards - 1)

    def fold(i, n):
        return jnp.where(lax.rem(i, 2) == 1, n // 2 - (i + 1) // 2, n // 2 + i // 2)

    def nth_peer(k):
        return at(x + fold(lax.rem(k, 2 * nx) // 2, nx), y + fold(k // (2 * nx), ny), lax.rem(core + 1 - lax.rem(k, 2), 2))

    def tell(k, c):
        remote(ids_all.at[me], ids_all.at[me], id_sems.at[0], id_sems.at[1], {"group": nth_peer(k)}).start()
        return c

    lax.fori_loop(0, groups - 1, tell, 0)
    loads[1].wait()
    loads[2].wait()
    neg_row = lax.rem(neg_v[...], rows_dev)
    neg_hot = hot(jnp.broadcast_to(neg_row, (rows_dev, nneg)) == iota((rows_dev, nneg), 0)).T
    drawn = select_dot(neg_hot, table_v[...])
    mine = rows8(me, nneg)
    panel[mine] = drawn * lax.rsqrt(rows_sum(drawn * drawn) + 1e-06)

    def pass_on(block, device):
        where = rows8(block, nneg)
        remote(panel.at[where], panel.at[where], neg_send, neg_recv.at[block], {"group": device}).start()

    def arrive(block):
        where = rows8(block, nneg)
        remote(panel.at[where], panel.at[where], neg_send, neg_recv.at[block], {"group": me}).wait_recv()

    sibling = at(x, y, 1 - core)

    def across_x(block):
        pass_on(block, at(x + 1, y, core))
        pass_on(block, at(x - 1, y, core))

    for dy in (1, -1, 2, -2):
        pass_on(me, at(x, y + dy, core))

    def told():
        where = pl.ds(0, groups - 1)
        return remote(ids_all.at[where], ids_all.at[where], id_sems.at[0], id_sems.at[1], {"group": me})

    across_x(me)
    pass_on(me, sibling)
    def step_y(dy, onward=()):
        block = at(x, y + dy, core)
        arrive(block)
        for to in onward:
            pass_on(block, at(x, y + to, core))
        across_x(block)
        pass_on(block, sibling)

    step_y(-1)
    step_y(1)
    step_y(-2, (2, 1))
    step_y(2, (-1,))
    told().wait_recv()

    def widen(g, c):
        expand[rows8(g)] = jnp.broadcast_to(ids_all[g], (8, count))
        return c

    lax.fori_loop(0, groups, widen, 0)
    col, row = iota((count, count), 1), iota((count, count), 0)
    lanes, subs = iota((slots, count), 1), lax.rem(iota((slots, count), 0), 8)
    asked = expand[...]
    here = asked // rows_dev == me
    earlier = hot(row < col)
    turn = jnp.dot(hot(here), earlier, preferred_element_type=F32).astype(jnp.int32)
    kept = jnp.where(here & (turn == lax.rem(subs, 4)), asked - me * rows_dev + 1, 0).astype(F32).astype(BF16)
    ones = jnp.ones((count, count), BF16)
    named = jnp.dot(kept, ones, preferred_element_type=F32).astype(jnp.int32)
    fits = named == lanes + 1
    serve = jnp.concatenate([hot(fits & (subs < 4)), hot(fits & (subs >= 4))], axis=1)
    half = width // 2
    stacked = jnp.concatenate([table_v[:, :half], table_v[:, half:]], axis=0)
    served[...] = select_dot(serve, stacked)

    def give(k, c):
        peer = nth_peer(k)
        remote(served.at[rows8(peer)], recv.at[rows8(me)], row_sems.at[0], row_sems.at[1], {"group": peer}).start()
        return c

    recv[rows8(me)] = served[rows8(me)]
    lax.fori_loop(0, groups - 1, give, 0)
    for dy in (-3, 3, -4):
        step_y(dy)
    order = [0, -1, 1, -2, 2, -3, 3, -4]

    def step_x(dy):
        for dx in (-1, 1):
            block = at(x + dx, y + dy, core)
            arrive(block)
            if (dy % 2 == 0) == (dx < 0):
                pass_on(block, at(x - dx, y, core))
            pass_on(block, sibling)

    step_x(order[0])
    ids = jnp.broadcast_to(ids_v[...], (count, count))
    ids_t = ids.T
    own_row, own_col = ids // rows_dev, ids_t // rows_dev
    same = own_row == own_col
    rank_col = jnp.sum(jnp.where(same & (col < row), 1, 0), axis=1, keepdims=True)
    rank_row = jnp.sum(jnp.where(same & (row < col), 1, 0), axis=0, keepdims=True)
    slot_col = own_col[:, :1] * 8 + rank_col
    slot_row = own_row[:1] * 8 + rank_row
    named_t = lax.dot_general(ones, kept, NT, preferred_element_type=F32).astype(jnp.int32)
    fits_t = named_t == iota((count, slots), 0) + 1
    subs_t = lax.rem(iota((count, slots), 1), 8)
    picks[0] = hot(fits_t & (subs_t < 4))
    picks[1] = hot(fits_t & (subs_t >= 4))
    slot_sub = iota((slots, count), 0)
    place[:, :count] = hot(slot_sub == slot_row)
    place[:, count:] = hot(slot_sub == slot_row + 4)
    for load in loads[3:]:
        load.wait()
    step_x(order[1])

    def refine(source, high, low):
        def body(i, c):
            where = rows8(i, 32)
            high[where], low[where] = weights_of(source[where])
            return c

        lax.fori_loop(0, width // 32, body, 0)

    refine(w_in_v, in_hi, in_lo)
    step_x(order[2])
    refine(w_out_v, out_hi, out_lo)
    times = jnp.broadcast_to(time_v[...], (count, count))
    gap[...] = jnp.abs(times - times.T)
    buckets = rab_s.shape[1]
    for b in range(4):
        where = slice(b * count // 4, (b + 1) * count // 4)
        gaps = gap[where]

        def look(d, sums):
            for e in range(4):
                here = gaps == d * 4 + e
                sums = tuple(jnp.where(here, rab_s[n, d * 4 + e], s) for n, s in enumerate(sums))
            return sums

        found = lax.fori_loop(0, buckets // 4, look, (jnp.zeros(gaps.shape, F32),) * heads)
        for n in range(heads):
            bias[n, where] = found[n]
        step_x(order[3 + b])
    seg_row, seg_col = jnp.zeros((count, count), jnp.int32), jnp.zeros((count, count), jnp.int32)
    place_col = iota((count, 1), 0)
    valid = jnp.ones((count, 1), F32)
    end = 0
    for s in range(len_s.shape[1]):
        end = end + len_s[0, s]
        seg_row += jnp.where(col >= end, 1, 0)
        seg_col += jnp.where(row >= end, 1, 0)
        valid = jnp.where(place_col + 1 == end, 0.0, valid)
    allowed = jnp.where((col <= row) & (seg_row == seg_col), 1.0 / MOST_LEN, 0.0)
    valid = jnp.where(place_col + 1 == count, 0.0, valid)

    for dy in order[7:]:
        step_x(dy)

    def given():
        return remote(
            served.at[pl.ds(0, (groups - 1) * 8)], recv.at[pl.ds(0, (groups - 1) * 8)], row_sems.at[0], row_sems.at[1],
            {"group": me},
        )

    given().wait_recv()
    slot_lane = iota((count, slots), 1)
    for q in range(2):
        emb[:, q * half : (q + 1) * half] = select_dot(hot(slot_lane == slot_col + 4 * q), recv[...])
    e = emb[...]
    e = e - rows_sum(e) / width
    scale1 = lax.rsqrt(rows_sum(e * e) / width + 1e-05)
    norm[...] = e * scale1
    for c in range(4):
        part_c = slice(c * width, (c + 1) * width)
        pre = mul3(norm[...], in_hi[:, part_c], in_lo[:, part_c]) + b_in_v[:, part_c]
        sig = 1.0 / (1.0 + jnp.exp(-pre))
        hid[:, part_c] = pre * sig
        slope[:, part_c] = sig * (1.0 + pre * (1.0 - sig))
    for dy in order:
        block = at(x + 2, y + dy, core)
        arrive(block)
        pass_on(block, sibling)
    size = width // heads
    root = size ** (-0.5)

    def head(part_c, n):
        return slice(part_c * width + n * size, part_c * width + (n + 1) * size)

    for n in range(heads):
        score = mul3(hid[:, head(2, n)], *weights_of(hid[:, head(3, n)]), NT) * root + bias[n]
        sig = 1.0 / (1.0 + jnp.exp(-score))
        weight = score * sig * allowed
        attn[n] = weight
        attn_slope[n] = sig * (1.0 + score * (1.0 - sig)) * allowed
        mixed[:, head(0, n)] = mul3(weight, *weights_of(hid[:, head(1, n)]))
    m = mixed[...]
    m = m - rows_sum(m) / width
    scale2 = lax.rsqrt(rows_sum(m * m) / width + 1e-05)
    mixed[...] = m * scale2
    out = mul3(mixed[...] * hid[:, :width], out_hi[...], out_lo[...]) + emb[...]
    scale3 = lax.rsqrt(rows_sum(out * out) + 1e-06)
    state = out * scale3
    e = emb[...]
    row_col = iota((count, width), 0)
    after = jnp.where(row_col == count - 1, 0.0, pltpu.roll(e, count - 1, 0))
    scale4 = lax.rsqrt(rows_sum(after * after) + 1e-06)
    target = after * scale4
    positive = rows_sum(state * target) / TEMPER
    zneg = jnp.zeros((count, 1), F32)
    pulled = jnp.zeros((count, width), F32)
    state_hi, state_lo = weights_of(state)
    state_two = jnp.concatenate([state_hi, state_lo], axis=0)
    for dx in (0, -1, 1, 2):
        for dy in range(ny):
            arrive(at(x + dx, y + dy, 1 - core))
        block = panel[rows8(lax.rem(x + dx + nx, nx), 2 * ny * nneg)]
        high, low = weights_of(block)
        logit = lax.dot_general(state_two, high, NT, preferred_element_type=F32)
        logit = logit[:count] + logit[count:] + lax.dot_general(state_hi, low, NT, preferred_element_type=F32)
        exps = jnp.exp(logit / TEMPER)
        zneg += rows_sum(exps)
        pulled += mul3(exps, high, low)
    expos = jnp.exp(positive)
    total = expos + zneg
    loss = valid * (jnp.log(total) - positive)
    loss_ref[...] = jnp.broadcast_to(loss, (count, count)).T[:1]
    share = expos / total - 1.0
    weigh = valid / TEMPER
    d_state = weigh * (share * target + pulled / total)
    d_target = (weigh * share) * state
    d_out = scale3 * (d_state - state * rows_sum(state * d_state))
    d_after = scale4 * (d_target - target * rows_sum(target * d_target))
    d_emb = d_out + jnp.where(row_col == 0, 0.0, pltpu.roll(d_after, 1, 0))
    emb[...] = d_emb
    d_gated = mul3(d_out, out_hi[...], out_lo[...], NT)
    dhid[:, :width] = d_gated * mixed[...] * slope[:, :width]
    mixed[...] = norm_back(d_gated * hid[:, :width], mixed[...], scale2)
    for n in range(heads):
        d_mix = mixed[:, head(0, n)]
        weight = attn[n]
        d_weight = mul3(d_mix, *weights_of(hid[:, head(1, n)]), NT)
        d_score = d_weight * attn_slope[n] * root
        mix_hi, mix_lo = weights_of(d_mix)
        dhid[:, head(1, n)] = mul3(weight.T, mix_hi, mix_lo) * slope[:, head(1, n)]
        dhid[:, head(2, n)] = mul3(d_score, *weights_of(hid[:, head(3, n)])) * slope[:, head(2, n)]
        dhid[:, head(3, n)] = mul3(d_score.T, *weights_of(hid[:, head(2, n)])) * slope[:, head(3, n)]
    d_norm = mul3(dhid[:, :width], in_hi[:, :width], in_lo[:, :width], NT)
    for c in range(1, 4):
        part_c = slice(c * width, (c + 1) * width)
        d_norm += mul3(dhid[:, part_c], in_hi[:, part_c], in_lo[:, part_c], NT)
    emb[...] += norm_back(d_norm, norm[...], scale1)
    chunks = outgoing.shape[0]
    last = shards - 1
    z_order = sorted(range(1, shards), key=lambda k: -min(k, shards - k))
    for h in range(chunks):
        cols = [slice((2 * h + q) * 128, (2 * h + q + 1) * 128) for q in range(2)]
        outgoing[h] = select_dot(place[...], jnp.concatenate([emb[:, c] for c in cols], axis=0))

        def send(k, c):
            peer = nth_peer(k)
            remote(
                outgoing.at[h, rows8(peer)], incoming.at[h, rows8(me)], send_sem.at[h], recv_sem.at[h], {"group": peer}
            ).start()
            return c

        lax.fori_loop(0, groups - 1, send, 0)
        incoming[h, rows8(me)] = outgoing[h, rows8(me)]

    def whole(h):
        where = pl.ds(0, (groups - 1) * 8)
        return remote(outgoing.at[h, where], incoming.at[h, where], send_sem.at[h], recv_sem.at[h], {"group": me})

    for h in range(chunks):
        whole(h).wait_recv()
        spare = part.shape[1] - 2 * 128
        part[h, pl.ds(2 * 128, spare)] = jnp.zeros((spare, 128), F32)
        for q in range(2):
            part[h, pl.ds(q * 128, 128)] = select_dot(picks[q], incoming[h])

        for k in z_order:
            peer = lax.rem(my + k, shards)

            @pl.when(peer != last)
            def _():
                remote(
                    part.at[h, rows8(peer, piece)], rsum.at[h, my], rs_send.at[h], rs_recv.at[h], {"shard": peer}
                ).start()

        rsum[h, my] = part[h, rows8(my, piece)]

    def some_rs(h, pieces):
        where = pl.ds(0, pieces)
        return remote(rsum.at[h, where], rsum.at[h, where], rs_send.at[h], rs_recv.at[h], {"shard": my})

    def some_red(h, pieces):
        where = pl.ds(0, pieces * piece)
        return remote(red_ref.at[h, where], red_ref.at[h, where], ag_send.at[h], ag_recv.at[h], {"shard": my})

    own = rows8(my, piece)
    for h in range(chunks):

        @pl.when(my != last)
        def _():
            some_rs(h, shards - 1).wait_recv()
            red_ref[h, own] = jnp.sum(rsum[h], axis=0)
            for k in z_order:
                peer = lax.rem(my + k, shards)
                remote(red_ref.at[h, own], red_ref.at[h, own], ag_send.at[h], ag_recv.at[h], {"shard": peer}).start()

    for h in range(chunks):

        @pl.when(my != last)
        def _():
            some_red(h, shards - 2).wait_recv()
            some_red(h, shards - 1).wait_send()
            some_rs(h, shards - 2).wait_send()

        @pl.when(my == last)
        def _():
            some_red(h, shards - 1).wait_recv()
            some_rs(h, shards - 1).wait_send()

        whole(h).wait_send()
    told().wait_send()
    given().wait_send()
    sent = pl.ds(0, (groups - 1) * nneg)
    remote(panel.at[sent], panel.at[sent], neg_send, neg_recv.at[0], {"group": me}).wait_send()


def settle_kernel(red_ref, loss_in, grad_ref, loss_ref):
    count = grad_ref.shape[0]
    for q in range(grad_ref.shape[1] // 128):
        grad_ref[:, q * 128 : (q + 1) * 128] = red_ref[q // 2, q % 2 * count : (q % 2 + 1) * count]
    loss_ref[...] = loss_in[...]


def body(item_ids, seq_lengths, time_buckets, neg_ids, table, w_in, b_in, w_out, rab):
    groups, shards = lax.axis_size("group"), lax.axis_size("shard")
    count, width = item_ids.shape[0], table.shape[1]
    heads, hidden = rab.shape[0], w_in.shape[1]
    nneg = neg_ids.shape[1]
    slots, chunks = groups * 8, width // 256
    piece = (-(-256 // shards) + 7) // 8 * 8
    red_rows = shards * piece
    vm, smem, dma, i32 = pltpu.VMEM, pltpu.SMEM, pltpu.SemaphoreType.DMA, jnp.int32
    anywhere = pl.BlockSpec(memory_space=pl.ANY)
    red, loss = pl.pallas_call(
        functools.partial(step_kernel, (groups // 16, 8), shards, piece, heads),
        out_shape=(
            jax.ShapeDtypeStruct((chunks, red_rows, 128), F32),
            jax.ShapeDtypeStruct((1, count), F32),
        ),
        in_specs=[anywhere] * 9,
        out_specs=(pl.BlockSpec(memory_space=vm),) * 2,
        scratch_shapes=[
            vm((1, count), i32),
            smem(seq_lengths.shape, i32),
            vm((1, count), i32),
            vm((1, nneg), i32),
            vm(table.shape, F32),
            vm(w_in.shape, F32),
            vm((1, hidden), F32),
            vm(w_out.shape, F32),
            smem(rab.shape, F32),
            dma((9,)),
            vm(w_in.shape, BF16),
            vm(w_in.shape, BF16),
            vm(w_out.shape, BF16),
            vm(w_out.shape, BF16),
            vm((groups * nneg, width), F32),
            vm((groups, 1, count), i32),
            vm((slots, count), i32),
            vm((slots, width // 2), F32),
            vm((slots, width // 2), F32),
            vm((slots, 2 * count), BF16),
            vm((2, count, slots), BF16),
            vm((count, width), F32),
            vm((count, width), F32),
            vm((count, hidden), F32),
            vm((count, hidden), F32),
            vm((count, count), i32),
            vm((heads, count, count), F32),
            vm((heads, count, count), F32),
            vm((heads, count, count), F32),
            vm((count, width), F32),
            vm((count, hidden), F32),
            vm((chunks, slots, 128), F32),
            vm((chunks, slots, 128), F32),
            vm((chunks, red_rows, 128), F32),
            vm((chunks, shards, piece, 128), F32),
            dma((2,)),
            dma((2,)),
            dma,
            dma((groups,)),
        ]
        + [dma((chunks,))] * 6,
        compiler_params=pltpu.CompilerParams(collective_id=0, has_side_effects=True, vmem_limit_bytes=56 << 20),
        name="hstu_step",
    )(
        item_ids.reshape(1, -1), seq_lengths, time_buckets.reshape(1, -1), neg_ids, table, w_in, b_in.reshape(1, -1), w_out,
        rab,
    )
    inside = pl.BlockSpec(memory_space=vm)
    grad, loss = pl.pallas_call(
        settle_kernel,
        out_shape=(jax.ShapeDtypeStruct((count, width), F32), jax.ShapeDtypeStruct((1, count), F32)),
        in_specs=[inside] * 2,
        out_specs=(inside,) * 2,
        name="settle",
    )(red, loss)
    return grad, loss.reshape(-1)


def solution(mesh):
    in_specs = (
        P(("shard", "group")),
        P(("shard", "group"), None),
        P(("shard", "group")),
        P("shard", "group"),
        P("group", None),
        P(),
        P(),
        P(),
        P(),
    )
    out_specs = (P("group", None), P(("shard", "group")))
    return jax.shard_map(body, mesh=mesh, in_specs=in_specs, out_specs=out_specs, check_vma=False)
```
